32 devices in a mesh: section: 2 (over y), dp: 4 (over x, core), tensor: 4 (over z).
Axes of the slice: x: 2, y: 2, z: 4, core: 2. Of those that a mesh axis runs over, the one named last changes fastest.
Arguments:
- master_weight: float32 [2304, 128, 128], P(('section', 'tensor'), 'dp'), parts along dimension 0, may hold values from -6 to 6
- first_moment: float32 [2304, 128, 128], P(('section', 'tensor'), 'dp'), parts along dimension 0, may hold values from -2 to 2
- second_moment: float32 [2304, 128, 128], P(('section', 'tensor'), 'dp'), parts along dimension 0, may hold values from 0.01 to 1
- grads: bfloat16 [4, 2304, 128, 128], P('dp', ('section', 'tensor')), parts along dimension 1, may hold values from -6 to 6
- dest_table: int32 [1152], replicated, may hold values from 0 to 1151, as said below
Outputs:
- weight_new: float32 [2304, 128, 128], P(('section', 'tensor'), 'dp'), parts along dimension 0
- first_new: float32 [2304, 128, 128], P(('section', 'tensor'), 'dp'), parts along dimension 0
- second_new: float32 [2304, 128, 128], P(('section', 'tensor'), 'dp'), parts along dimension 0
- weights: bfloat16 [2304, 128, 128], P(('section', 'tensor')), parts along dimension 0
The draws below stay inside these ranges and needn't reach their ends.
There are 2 independent parts, one for each index of `section`. The reference program is written for one: setup_inputs(seed, part) draws one part's arguments, and reference() takes and returns one part's arrays. A program takes and returns all parts, laid end to end along the dimension named above; an argument that names none is the same for every part. Nothing has to cross between parts.
Inputs may be any that keep to these rules, and one draw needn't show every extreme that they name: `dest_table`: A permutation. Group old slots by s // 288 and new positions by p // 288: at most 72 slots of one group have positions in one block, and some pair of group and block has exactly 72.
All inputs are finite; a program needn't handle non-finite values.
Results may differ from the reference program's by a relative error of at most 0.0023.
Values may be sent and summed in bfloat16 or wider, within the bound.
A program may use at most 128 MiB of HBM per device.

```python
import math
import jax
import jax.numpy as jnp
from jax import lax

HD = 128
STEP = 10
TILES = 1152
TPD = 288
TROWS = 128
N_DP = 4


def draw_dest_table(key, part):
    groups = TILES // TPD
    key_shift = jax.random.fold_in(key, 11)
    key_order = jax.random.fold_in(key, 23)
    shifts = jax.random.permutation(key_shift, groups).astype(jnp.int32)
    slot_ids = jnp.arange(TILES, dtype=jnp.int32)
    source = slot_ids // TPD
    within = slot_ids % TPD
    target = (shifts[source] + within // 2) % groups
    mixing = jax.random.permutation(key_order, TILES).astype(jnp.int32)
    ordered = jnp.argsort(target * TILES + mixing, stable=True)
    return jnp.argsort(ordered, stable=True).astype(jnp.int32)


def raised(drawn, stream_key, source, target, parts, factor):
    def block_of(dim):
        return (jnp.arange(drawn.shape[dim]) // (drawn.shape[dim] // parts)).reshape((-1,) + (1,) * (drawn.ndim - 1 - dim))

    one_side = jax.random.permutation(stream_key, parts)[block_of(target)]
    second = (block_of(target) + parts // 2) % parts
    return jnp.where((block_of(source) == one_side) | (block_of(source) == second), factor * drawn, drawn)


def levels(rng, shape, shards, low, high):
    loudness, own = 1.0, jax.random.fold_in(rng, 6)
    for dim, parts in shards:
        heights = jnp.exp(jax.random.uniform(jax.random.fold_in(own, dim), (parts,), jnp.float32, low / len(shards), high / len(shards)))
        loudness = loudness * jnp.repeat(heights, shape[dim] // parts).reshape([-1 if axis == dim else 1 for axis in range(len(shape))])
    return loudness


def scatter_about(key, extent, spread, limit, split=(), kind=jnp.bfloat16):
    array = jax.random.normal(key, extent, jnp.float32) * spread
    if len(split) > 0:
        array = levels(key, extent, split, -0.22, 0.18) * array
    return jnp.clip(array, min=-limit, max=limit).astype(kind)


def noise_with(key, dims, spread, most, split, heavy, kind=jnp.bfloat16):
    drawn = spread * jax.random.normal(key, dims, jnp.float32)
    if split:
        drawn = drawn * levels(key, dims, split, -0.22, 0.18)
    return jnp.clip(raised(drawn, jax.random.fold_in(key, 3), *heavy), -most, most).astype(kind)


def setup_inputs(seed: int = 0, part: int = 0) -> dict:
    splits = jax.random.split(jax.random.key(seed), 6)
    part_keys = jax.random.split(jax.random.fold_in(splits[5], part), 6)
    return {
        "master_weight": scatter_about(part_keys[0], (TILES, TROWS, HD), 1.0, 6.0, ((0, 4), (1, 4)), jnp.float32),
        "first_moment": scatter_about(part_keys[1], (TILES, TROWS, HD), 0.3, 2.0, ((0, 4), (1, 4)), jnp.float32),
        "second_moment": jnp.clip(jnp.exp(math.log(1.0) - 4.6051702 * jax.random.uniform(part_keys[2], (TILES, TROWS, HD), jnp.float32) ** levels(part_keys[2], (TILES, TROWS, HD), ((0, 4), (1, 4)), -0.2, 0.2)), 0.01, 1.0),
        "grads": noise_with(part_keys[3], (N_DP, TILES, TROWS, HD), 1.0, 6.0, ((0, 4), (1, 4)), (0, 2, 4, 2.0)),
        "dest_table": draw_dest_table(jax.random.fold_in(splits[5], 71), part),
    }


learn_rate = 0.04
decay_rate = 1.5
beta_first = 0.9
beta_second = 0.95
epsilon = 1e-08

def adam_step(weight, first, second, grad):
    first_new = beta_first * first + (1.0 - beta_first) * grad
    second_new = beta_second * second + (1.0 - beta_second) * grad * grad
    first_hat = first_new / (1.0 - beta_first ** STEP)
    second_hat = second_new / (1.0 - beta_second ** STEP)
    weight_new = weight - learn_rate * (first_hat / (jnp.sqrt(second_hat) + epsilon) + decay_rate * weight)
    return (weight_new, first_new, second_new)

def reference(master_weight, first_moment, second_moment, grads, dest_table):

    def placed(values):
        return jnp.zeros_like(values).at[dest_table].set(values)
    grad = lax.optimization_barrier(jnp.sum(grads.astype(jnp.float32), axis=0)) / grads.shape[0]
    weight_new, first_new, second_new = adam_step(placed(master_weight), placed(first_moment), placed(second_moment), grad)
    return (weight_new, first_new, second_new, weight_new.astype(jnp.bfloat16))
```

```python
import functools
import math

import jax
import jax.numpy as jnp
from jax import lax
from jax.experimental import pallas as pl
from jax.experimental.pallas import tpu as pltpu
from jax.sharding import PartitionSpec as P

STEP = 10


learn_rate = 0.04
decay_rate = 1.5
beta_first = 0.9
beta_second = 0.95
epsilon = 1e-08


def adam_step(weight, first, second, grad):
    first_new = beta_first * first + (1.0 - beta_first) * grad
    second_new = beta_second * second + (1.0 - beta_second) * grad * grad
    first_hat = first_new * (1.0 / (1.0 - beta_first**STEP))
    second_hat = second_new * (1.0 / (1.0 - beta_second**STEP))
    weight_new = weight - learn_rate * (
        first_hat / (jnp.sqrt(second_hat) + epsilon) + decay_rate * weight
    )
    return (weight_new, first_new, second_new)


def routes(dest_table, slots, groups, capacity, rank_here):
    total = dest_table.shape[0]
    length = groups * capacity
    target = dest_table // slots
    local = dest_table % slots
    layout = target.reshape(groups, slots)
    order = jnp.arange(slots, dtype=jnp.int32)
    same = (layout[:, :, None] == layout[:, None, :]) & (order[None, :] < order[:, None])[None]
    within = jnp.sum(same.astype(jnp.int32), axis=2).reshape(total)
    source = jnp.arange(total, dtype=jnp.int32) // slots
    leaving = lax.dynamic_slice_in_dim(target * capacity + within, rank_here * slots, slots)
    places = jnp.arange(length, dtype=jnp.int32)
    outgoing = jnp.sum(jnp.where(leaving[None, :] == places[:, None], order[None, :], 0), axis=1)
    coming = jnp.where(target == rank_here, source * capacity + within, length)
    landing = jnp.sum(jnp.where(coming[None, :] == places[:, None], local[None, :] + 1, 0), axis=1)
    return (outgoing, landing - 1)


ROWS = 8
SCALE = 8192.0
SPARE = 256 * 1024
CUTS = 4
FEW = 8
MESH = pl.DeviceIdType.MESH


def encode(weight):
    scaled = weight * SCALE
    square = scaled * scaled
    fourth = square * square
    return (scaled * jnp.abs(scaled) * square * fourth).astype(jnp.bfloat16)


def decode(code):
    wide = code.astype(jnp.float32)
    root = jnp.sqrt(jnp.sqrt(jnp.sqrt(jnp.abs(wide)))) * (1.0 / SCALE)
    return jnp.where(wide < 0.0, -root, root)


def flipped(index, mask):
    for bit in range(mask.bit_length()):
        if mask >> bit & 1:
            index = index + (1 - 2 * lax.rem(index // 2**bit, 2)) * 2**bit
    return index


def loop(start, size, body):
    lax.fori_loop(0, size, lambda i, carry: (body(start + i), carry)[1], 0, unroll=math.gcd(size, 8))


def exchange_kernel(
    groups, replicas, capacity, chunks,
    outgoing, landing, weight, first, second, grads,
    weight_new, first_new, second_new, weights,
    raw, sent, got, own_here, own_far, twin_here, twin_far, far_here,
    load_sem, own_sem, wide_send, wide_recv, twin_send, twin_recv, far_send, far_recv,
    last_send, last_recv, relay_send,
):
    slots, rows = weight.shape[0], weight.shape[1]
    me = lax.axis_index("tensor")
    mine = lax.axis_index("dp")
    chips = replicas // 2
    core = lax.rem(mine, 2)
    twin = mine + 1 - 2 * core
    across = range(1, chips)
    power = groups & (groups - 1) == 0
    fine = groups <= FEW
    cuts = CUTS if fine and capacity % CUTS == 0 else 1
    hops = range(groups - 1, 0, -1)

    def partner(k):
        return flipped(me, k) if power else lax.rem(me + k, groups)

    def giver(k):
        return flipped(me, k) if power else lax.rem(me + groups - k, groups)

    def far(k):
        return lax.rem(mine + 2 * k, replicas)

    def far_twin(k):
        return lax.rem(mine + 2 * k, replicas) + 1 - 2 * core

    def band(chunk, owner=None):
        if owner is None:
            return pl.ds(chunk * ROWS, ROWS)
        return pl.ds(pl.multiple_of(owner * rows + chunk * ROWS, ROWS), ROWS)

    def pieces(chunk):
        return cuts if chunk == chunks - 1 else 1

    def loads(chunk):
        return [
            pltpu.make_async_copy(
                ref.at[:, band(chunk), :], raw[chunk % 2].at[k], load_sem.at[chunk % 2, k]
            )
            for k, ref in enumerate((weight, first, second))
        ]

    def wide(chunk, piece, k, source, target):
        size = capacity // pieces(chunk)
        return pltpu.make_async_remote_copy(
            src_ref=sent.at[chunk, :, pl.ds(target * capacity + piece * size, size)],
            dst_ref=got[chunk].at[:, pl.ds(source * capacity + piece * size, size)],
            send_sem=wide_send.at[chunk, piece, k],
            recv_sem=wide_recv.at[chunk, piece, k],
            device_id={"tensor": target},
            device_id_type=MESH,
        )

    def grad_loads(chunk):
        return [
            pltpu.make_async_copy(
                grads.at[0, :, band(chunk, far(k)), :], own_far.at[chunk, k - 1], own_sem.at[chunk, k]
            )
            if k
            else pltpu.make_async_copy(
                grads.at[0, :, band(chunk, mine), :], own_here[chunk], own_sem.at[chunk, 0]
            )
            for k in range(chips)
        ]

    def twin_copy(chunk, k):
        return pltpu.make_async_remote_copy(
            src_ref=grads.at[0, :, band(chunk, far_twin(k)), :],
            dst_ref=twin_far.at[chunk, k - 1] if k else twin_here[chunk],
            send_sem=twin_send.at[chunk, k],
            recv_sem=twin_recv.at[chunk, k],
            device_id={"dp": twin},
            device_id_type=MESH,
        )

    def far_copy(chunk, k):
        return pltpu.make_async_remote_copy(
            src_ref=own_far.at[chunk, k - 1],
            dst_ref=far_here[chunk][chips - k - 1],
            send_sem=far_send.at[chunk, k],
            recv_sem=far_recv.at[chunk, chips - k],
            device_id={"dp": far(k)},
            device_id_type=MESH,
        )

    def far_wait(chunk, k):
        return pltpu.make_async_remote_copy(
            src_ref=own_far.at[chunk, chips - k - 1],
            dst_ref=far_here[chunk][k - 1],
            send_sem=far_send.at[chunk, chips - k],
            recv_sem=far_recv.at[chunk, k],
            device_id={"dp": far(k)},
            device_id_type=MESH,
        )

    def steps(chunk):
        if not fine:
            return [([(0, k) for k in hops], 0, groups * capacity)]
        size = capacity // pieces(chunk)
        found = [([], me * capacity, capacity)]
        if pieces(chunk) > 1:
            found.append(([(i, 1) for i in range(pieces(chunk))], giver(1) * capacity, capacity))
            for i in range(pieces(chunk)):
                for k in range(groups - 1, 1, -1):
                    found.append(([(i, k)], giver(k) * capacity + i * size, size))
        else:
            for k in hops:
                found.append(([(0, k)], giver(k) * capacity, capacity))
        return found

    def spread(chunk, step, owner, target, send):
        _, start, size = steps(chunk)[step]
        here = weights.at[pl.ds(start, size), band(chunk, owner), :]
        return pltpu.make_async_remote_copy(
            src_ref=here,
            dst_ref=here,
            send_sem=send.at[chunk, step, lax.div(target, 2) if send is last_send else lax.div(owner, 2)],
            recv_sem=last_recv.at[chunk, step, owner],
            device_id={"dp": target},
            device_id_type=MESH,
        )

    def start(copies):
        for copy in copies:
            copy.start()

    def finish(copies):
        for copy in copies:
            copy.wait()

    start(loads(0))
    barrier = pltpu.get_barrier_semaphore()
    for k in hops:
        pl.semaphore_signal(barrier, inc=1, device_id={"tensor": partner(k)}, device_id_type=MESH)
    pl.semaphore_signal(barrier, inc=1, device_id={"dp": twin}, device_id_type=MESH)
    for k in across:
        pl.semaphore_signal(barrier, inc=1, device_id={"dp": far(k)}, device_id_type=MESH)
    for chunk in range(chunks):
        start(grad_loads(chunk))
    if chunks > 1:
        start(loads(1))

    def pack(chunk, target, source_of=None):
        def one(j):
            s = outgoing[j]
            place = j if source_of is None else source_of
            values = (
                encode(raw[chunk % 2][0, s]),
                raw[chunk % 2][1, s].astype(jnp.bfloat16),
                raw[chunk % 2][2, s].astype(jnp.bfloat16),
            )
            for k, value in enumerate(values):
                if source_of is None:
                    sent[chunk, k, j] = value
                else:
                    got[chunk][k, j] = value

        loop(target * capacity, capacity, one)

    waiting = []

    def send(copies):
        start(waiting)
        waiting[:] = copies

    for chunk in range(chunks):
        finish(loads(chunk))
        last = pieces(chunk) > 1
        for k in [1] * last + [k for k in hops if k > 1 or not last]:
            pack(chunk, partner(k))
            if chunk == 0 and k == groups - 1:
                pl.semaphore_wait(barrier, groups - 1 + chips)
                for other in range(chunks):
                    start([twin_copy(other, i) for i in reversed(range(chips))])
            if not last:
                send([wide(chunk, 0, k, me, partner(k))])
            elif k == 1:
                send([wide(chunk, i, 1, me, partner(1)) for i in range(cuts)])
        if last:
            send([
                wide(chunk, i, k, me, partner(k)) for i in range(cuts) for k in hops if k > 1
            ])
        pack(chunk, me, me)
        if chunk + 2 < chunks:
            start(loads(chunk + 2))
        send([])
        finish(grad_loads(chunk))
        for k in across:
            twin_copy(chunk, k).wait_recv()

            def join(s, chunk=chunk, k=k):
                total = own_far[chunk, k - 1, s].astype(jnp.float32) + twin_far[chunk, k - 1, s].astype(jnp.float32)
                own_far[chunk, k - 1, s] = total.astype(jnp.bfloat16)

            loop(0, slots, join)
            far_copy(chunk, k).start()

    def relay(chunk, step):
        for k in across:
            spread(chunk, step, far(k), twin, relay_send).wait_recv()
            spread(chunk, step, far(k), twin, relay_send).start()

    behind = []
    for chunk in range(chunks):
        twin_copy(chunk, 0).wait_recv()
        for k in across:
            far_wait(chunk, k).wait_recv()

        def update(j, chunk=chunk):
            p = jnp.maximum(landing[j], 0)
            grad = own_here[chunk][p].astype(jnp.float32) + twin_here[chunk][p].astype(jnp.float32)
            for k in across:
                grad = grad + far_here[chunk][k - 1][p].astype(jnp.float32)
            weight_here, first_here, second_here = adam_step(
                decode(got[chunk][0, j]),
                got[chunk][1, j].astype(jnp.float32),
                got[chunk][2, j].astype(jnp.float32),
                grad * (1.0 / replicas),
            )
            weights[j, band(chunk, mine)] = weight_here.astype(jnp.bfloat16)
            weight_new[j, band(chunk)] = weight_here
            first_new[j, band(chunk)] = first_here
            second_new[j, band(chunk)] = second_here

        for step, (waits, base, size) in enumerate(steps(chunk)):
            for piece, k in waits:
                wide(chunk, piece, k, giver(k), me).wait_recv()
            loop(base, size, update)
            start([spread(chunk, step, mine, far(k), last_send) for k in across])
            spread(chunk, step, mine, twin, last_send).start()
            behind.append((chunk, step))
            while len(behind) > 4:
                relay(*behind.pop(0))
    for chunk, step in behind:
        relay(chunk, step)

    for chunk in range(chunks):
        for step in range(len(steps(chunk))):
            spread(chunk, step, twin, twin, last_send).wait_recv()
            spread(chunk, step, mine, twin, last_send).wait_send()
            for k in across:
                spread(chunk, step, mine, far(k), last_send).wait_send()
                spread(chunk, step, far(k), twin, relay_send).wait_send()
                spread(chunk, step, far_twin(k), twin, relay_send).wait_recv()
    for chunk in range(chunks):
        for k in range(chips):
            twin_copy(chunk, k).wait_send()
        for k in across:
            far_copy(chunk, k).wait_send()
        for k in hops:
            for piece in range(pieces(chunk)):
                wide(chunk, piece, k, me, partner(k)).wait_send()


def place_kernel(landing, weight, first, second, weights, weight_new, first_new, second_new, weights_new, sem):
    length, slots = weight.shape[0], weight_new.shape[0]
    pairs = ((weight, weight_new), (first, first_new), (second, second_new), (weights, weights_new))

    def one(j, carry):
        p = landing[j]

        def move():
            for k, (source, target) in enumerate(pairs):
                pltpu.make_async_copy(source.at[j], target.at[p], sem.at[k]).start()

        if length == slots:
            move()
        else:
            pl.when(p >= 0)(move)
        return carry

    lax.fori_loop(0, length, one, 0, unroll=math.gcd(length, 8))
    for k, (source, target) in enumerate(pairs):
        pltpu.make_async_copy(source.at[pl.ds(0, slots)], target, sem.at[k]).wait()


def exchange(outgoing, landing, weight, first, second, grads, groups, replicas, capacity):
    slots, rows, lanes = weight.shape
    chunks = rows // ROWS
    chips = replicas // 2
    length = groups * capacity
    anywhere = pl.BlockSpec(memory_space=pl.ANY)
    near = pl.BlockSpec(memory_space=pltpu.VMEM)
    table = pl.BlockSpec(memory_space=pltpu.SMEM)
    dma = pltpu.SemaphoreType.DMA
    fine = groups <= FEW
    cuts = CUTS if fine and capacity % CUTS == 0 else 1
    most = 2 + (groups - 2) * cuts if fine else 1
    most = max(most, groups) if fine else 1
    half = jnp.bfloat16
    tile = ROWS * lanes
    scratch = (
        2 * 3 * slots * tile * 4
        + chunks * 2 * 3 * length * tile * 2
        + chunks * slots * tile * 2 * (2 + 3 * (chips - 1))
    )
    whole = pltpu.VMEM((length, rows, lanes), jnp.float32)
    results = pl.pallas_call(
        functools.partial(exchange_kernel, groups, replicas, capacity, chunks),
        out_shape=(whole, whole, whole, pltpu.VMEM((length,) + grads.shape[2:], half)),
        in_specs=[table, table] + [anywhere] * 4,
        out_specs=(near,) * 4,
        scratch_shapes=[
            [pltpu.VMEM((3, slots, ROWS, lanes), jnp.float32)] * 2,
            pltpu.VMEM((chunks, 3, length, ROWS, lanes), half),
            [pltpu.VMEM((3, length, ROWS, lanes), half)] * chunks,
            [pltpu.VMEM((slots, ROWS, lanes), half)] * chunks,
            pltpu.VMEM((chunks, chips - 1, slots, ROWS, lanes), half),
            [pltpu.VMEM((slots, ROWS, lanes), half)] * chunks,
            pltpu.VMEM((chunks, chips - 1, slots, ROWS, lanes), half),
            [[pltpu.VMEM((slots, ROWS, lanes), half)] * (chips - 1)] * chunks,
            dma((2, 3)),
            dma((chunks, chips)),
            dma((chunks, cuts, groups)),
            dma((chunks, cuts, groups)),
            dma((chunks, chips)),
            dma((chunks, chips)),
            dma((chunks, chips)),
            dma((chunks, chips)),
            dma((chunks, most, chips)),
            dma((chunks, most, replicas)),
            dma((chunks, most, chips)),
        ],
        compiler_params=pltpu.CompilerParams(
            collective_id=0, has_side_effects=True, vmem_limit_bytes=scratch + SPARE
        ),
        name="exchange",
    )(outgoing, landing, weight, first, second, grads)
    shape = jax.ShapeDtypeStruct(weight.shape, jnp.float32)
    return pl.pallas_call(
        place_kernel,
        out_shape=(shape, shape, shape, jax.ShapeDtypeStruct(grads.shape[1:], half)),
        in_specs=[table] + [anywhere] * 4,
        out_specs=(anywhere,) * 4,
        scratch_shapes=[dma((4,))],
        compiler_params=pltpu.CompilerParams(vmem_limit_bytes=SPARE),
        name="place",
    )(landing, *results)


def shards(master_weight, first_moment, second_moment, grads, dest_table):
    groups = lax.axis_size("tensor")
    rank_here = lax.axis_index("tensor")
    slots = master_weight.shape[0]
    capacity = 2 * ((slots + 2 * groups - 1) // (2 * groups))
    outgoing, landing = routes(dest_table, slots, groups, capacity, rank_here)
    replicas = lax.axis_size("dp")
    return exchange(
        outgoing, landing, master_weight, first_moment, second_moment, grads,
        groups, replicas, capacity,
    )


def solution(mesh):
    placed = (
        P(("section", "tensor"), "dp", None),
        P(("section", "tensor"), "dp", None),
        P(("section", "tensor"), "dp", None),
        P("dp", ("section", "tensor"), None, None),
        P(),
    )
    return jax.shard_map(
        shards,
        mesh=mesh,
        in_specs=placed,
        out_specs=(
            P(("section", "tensor"), "dp", None),
            P(("section", "tensor"), "dp", None),
            P(("section", "tensor"), "dp", None),
            P(("section", "tensor"), None, None),
        ),
        check_vma=False,
    )
```

```python
import functools
import math

import jax
import jax.numpy as jnp
from jax import lax
from jax.experimental import pallas as pl
from jax.experimental.pallas import tpu as pltpu
from jax.sharding import PartitionSpec as P

STEP = 10


learn_rate = 0.04
decay_rate = 1.5
beta_first = 0.9
beta_second = 0.95
epsilon = 1e-08


def adam_step(weight, first, second, grad):
    first_new = beta_first * first + (1.0 - beta_first) * grad
    second_new = beta_second * second + (1.0 - beta_second) * grad * grad
    first_hat = first_new * (1.0 / (1.0 - beta_first**STEP))
    second_hat = second_new * (1.0 / (1.0 - beta_second**STEP))
    weight_new = weight - learn_rate * (
        first_hat / (jnp.sqrt(second_hat) + epsilon) + decay_rate * weight
    )
    return (weight_new, first_new, second_new)


ROWS = 8
SCALE = 8192.0
SPARE = 512 * 1024
LANES = 128
HELD = 4096
LINE = 4
LAG = 4
MESH = pl.DeviceIdType.MESH


def encode(weight):
    scaled = weight * SCALE
    square = scaled * scaled
    fourth = square * square
    return (scaled * jnp.abs(scaled) * square * fourth).astype(jnp.bfloat16)


def decode(code):
    wide = code.astype(jnp.float32)
    root = jnp.sqrt(jnp.sqrt(jnp.sqrt(jnp.abs(wide)))) * (1.0 / SCALE)
    return jnp.where(wide < 0.0, -root, root)


def loop(start, size, body):
    lax.fori_loop(0, size, lambda i, carry: (body(start + i), carry)[1], 0, unroll=math.gcd(size, 8))


def rows_from(flat, groups, slots):
    width = LANES * pl.cdiv(slots, LANES)
    found = []
    for group in range(groups):
        first, extra = divmod(group * slots, LANES)
        count = pl.cdiv(extra + slots, LANES)
        row = [flat[first + i : first + i + 1] for i in range(count)]
        row = jnp.concatenate(row, axis=1) if count > 1 else row[0]
        if extra:
            row = pltpu.roll(row, count * LANES - extra, 1)
        found.append(row[:, :width])
    spare = -groups % 8
    if spare:
        found.append(jnp.zeros((spare, width), jnp.int32))
    return jnp.concatenate(found, axis=0)


def routes(flat, groups, slots, me):
    dest = rows_from(flat, groups, slots)
    width = dest.shape[1]
    lane = lax.broadcasted_iota(jnp.int32, dest.shape, 1)
    line = lax.broadcasted_iota(jnp.int32, dest.shape, 0)
    target = jnp.where((lane < slots) & (line < groups), 0, -groups)
    for group in range(1, groups):
        target = target + (dest >= group * slots).astype(jnp.int32)
    leaving = jnp.sum(jnp.where(line == me, target, 0), axis=0, keepdims=True)
    coming = jnp.where(target == me, 1, 0)
    going = jnp.where(leaving == line, 1, 0)
    table = jnp.concatenate([coming, going], axis=0)
    value = jnp.concatenate([dest - me * slots, lane], axis=0)
    lane = jnp.concatenate([lane, lane], axis=0)
    before = table
    step = 1
    while step < slots:
        before = before + jnp.where(lane >= step, pltpu.roll(before, step, 1), 0)
        step *= 2
    held = jnp.where(table > 0, value + 1 + HELD * (lane + 1 - before), 0)
    step = 1
    while step < slots:
        moved = jnp.where(jnp.bitwise_and(held, HELD * step) > 0, held, 0)
        held = held - moved + pltpu.roll(moved, width - step, 1)
        step *= 2
    return jnp.bitwise_and(held, HELD - 1) - 1


def cut_of(groups, capacity):
    if groups == LINE and capacity % 8 == 0 and capacity > 32:
        return (capacity - 32, 16, 8, 8)
    return (capacity,)


def schedule(groups, chunks, cuts):
    if groups != LINE:
        return [(chunk, None, 0) for chunk in range(chunks)]
    last = chunks - 1
    timed = []
    for chunk in range(chunks):
        timed.append((chunk + 1.6, chunk, 0, 0))
        timed.append((chunk + 2.0, chunk, 1, 0))
        for role, when in ((2, 2.3), (3, 3.7)):
            count = cuts if chunk == last else 1
            late = last + 10.0 * role if chunk == last else chunk * 2.0 + when
            timed += [(late + piece, chunk, role, piece) for piece in range(count)]
    return [entry[1:] for entry in sorted(timed)]


def exchange_kernel(
    groups, replicas, capacity, chunks,
    dest, weight, first, second, grads,
    weight_new, first_new, second_new, weights, table_out,
    table, flat,
    raw, sent, got, own_here, own_far, twin_here, twin_far, far_here,
    table_sem, load_sem, own_sem, wide_send, wide_recv, twin_send, twin_recv, far_send, far_recv,
    last_send, last_recv, twin_last, relay_send, relay_recv,
):
    slots, rows = weight.shape[0], weight.shape[1]
    me = lax.axis_index("tensor")
    mine = lax.axis_index("dp")
    chips = replicas // 2
    core = lax.rem(mine, 2)
    twin = mine + 1 - 2 * core
    across = range(1, chips)
    line = groups == LINE
    cuts = cut_of(groups, capacity)
    order = schedule(groups, chunks, len(cuts))
    if line:
        side = me // 2
        near = me + 1 - 2 * lax.rem(me, 2)
        targets = [3 - me, lax.rem(me + 2, 4), near]
        sources = [me, near, 3 - 3 * side, 2 - side]
    else:
        targets = [lax.rem(me + k, groups) for k in range(1, groups)]
        sources = [lax.rem(me + groups - k, groups) for k in range(groups)]

    def far(k):
        return lax.rem(mine + 2 * k, replicas)

    def far_twin(k):
        return lax.rem(mine + 2 * k, replicas) + 1 - 2 * core

    def band(chunk, owner=None):
        if owner is None:
            return pl.ds(chunk * ROWS, ROWS)
        return pl.ds(pl.multiple_of(owner * rows + chunk * ROWS, ROWS), ROWS)

    def loads(chunk):
        return [
            pltpu.make_async_copy(
                ref.at[:, band(chunk), :], raw[chunk % 2].at[k], load_sem.at[chunk % 2]
            )
            for k, ref in enumerate((weight, first, second))
        ]

    def loaded(chunk):
        return pltpu.make_async_copy(raw[chunk % 2], raw[chunk % 2], load_sem.at[chunk % 2])

    def cut(chunk, piece, split):
        if chunk == chunks - 1 and split:
            return sum(cuts[:piece]), cuts[piece]
        return 0, capacity

    def wide(chunk, piece, split, source, target):
        begin, size = cut(chunk, piece, split)
        return pltpu.make_async_remote_copy(
            src_ref=sent.at[chunk, :, pl.ds(target * capacity + begin, size)],
            dst_ref=got[chunk].at[:, pl.ds(source * capacity + begin, size)],
            send_sem=wide_send.at[chunk],
            recv_sem=wide_recv.at[chunk + piece, source],
            device_id={"tensor": target},
            device_id_type=MESH,
        )

    def wide_sent(chunk):
        everything = sent.at[chunk, :, pl.ds(0, (groups - 1) * capacity)]
        return pltpu.make_async_remote_copy(
            src_ref=everything,
            dst_ref=everything,
            send_sem=wide_send.at[chunk],
            recv_sem=wide_recv.at[chunk, 0],
            device_id={"tensor": targets[0]},
            device_id_type=MESH,
        )

    def grad_loads(chunk):
        return [
            pltpu.make_async_copy(
                grads.at[0, :, band(chunk, far(k)), :], own_far.at[chunk, k - 1], own_sem.at[chunk, k]
            )
            if k
            else pltpu.make_async_copy(
                grads.at[0, :, band(chunk, mine), :], own_here[chunk], own_sem.at[chunk, 0]
            )
            for k in range(chips)
        ]

    def twin_copy(chunk, k):
        return pltpu.make_async_remote_copy(
            src_ref=grads.at[0, :, band(chunk, far_twin(k)), :],
            dst_ref=twin_far.at[chunk, k - 1] if k else twin_here[chunk],
            send_sem=twin_send.at[k],
            recv_sem=twin_recv.at[chunk, k],
            device_id={"dp": twin},
            device_id_type=MESH,
        )

    def far_copy(chunk, k):
        return pltpu.make_async_remote_copy(
            src_ref=own_far.at[chunk, k - 1],
            dst_ref=far_here[chunk][chips - k - 1],
            send_sem=far_send.at[k],
            recv_sem=far_recv.at[chunk, chips - k],
            device_id={"dp": far(k)},
            device_id_type=MESH,
        )

    def far_wait(chunk, k):
        return pltpu.make_async_remote_copy(
            src_ref=own_far.at[chunk, chips - k - 1],
            dst_ref=far_here[chunk][k - 1],
            send_sem=far_send.at[chips - k],
            recv_sem=far_recv.at[chunk, k],
            device_id={"dp": far(k)},
            device_id_type=MESH,
        )

    def extent(entry):
        chunk, role, piece = entry
        if role is None:
            return 0, groups * capacity
        begin, size = cut(chunk, piece, role > 1)
        return sources[role] * capacity + begin, size

    def rows_of(entry):
        if entry[1] is None:
            return [(source, 0, capacity) for source in range(groups)]
        return [(sources[entry[1]], *cut(entry[0], entry[2], entry[1] > 1))]

    def spread(step, owner, target, send, recv):
        start, size = extent(order[step])
        here = weights.at[pl.ds(start, size), band(order[step][0], owner), :]
        return pltpu.make_async_remote_copy(
            src_ref=here,
            dst_ref=here,
            send_sem=send,
            recv_sem=recv,
            device_id={"dp": target},
            device_id_type=MESH,
        )

    def far_spread(step, k):
        return spread(step, mine, far(k), last_send.at[k], last_recv.at[step, chips - k - 1])

    def twin_spread(step):
        return spread(step, mine, twin, last_send.at[0], twin_last.at[0])

    def relay(step, k):
        return spread(step, far(k), twin, relay_send.at[k], relay_recv.at[k])

    def whole(owner, send, recv):
        here = weights.at[:, pl.ds(pl.multiple_of(owner * rows, ROWS), rows), :]
        return pltpu.make_async_remote_copy(
            src_ref=here,
            dst_ref=here,
            send_sem=send,
            recv_sem=recv,
            device_id={"dp": twin},
            device_id_type=MESH,
        )

    def every(ref, send, recv):
        return pltpu.make_async_remote_copy(
            src_ref=ref, dst_ref=ref, send_sem=send, recv_sem=recv,
            device_id={"dp": twin}, device_id_type=MESH,
        )

    def start(copies):
        for copy in copies:
            copy.start()

    fetch = pltpu.make_async_copy(dest, flat, table_sem.at[0])
    fetch.start()
    start(loads(0))
    barrier = pltpu.get_barrier_semaphore()
    for target in targets:
        pl.semaphore_signal(barrier, inc=1, device_id={"tensor": target}, device_id_type=MESH)
    pl.semaphore_signal(barrier, inc=1, device_id={"dp": twin}, device_id_type=MESH)
    for k in across:
        pl.semaphore_signal(barrier, inc=1, device_id={"dp": far(k)}, device_id_type=MESH)
    half = table_out.shape[0] // 2
    fetch.wait()
    table_out[...] = routes(flat[...], groups, slots, me)[:, : table_out.shape[1]]
    start(grad_loads(0))
    copy = pltpu.make_async_copy(table_out, table, table_sem.at[1])
    copy.start()
    copy.wait()

    def pack(chunk, target, to_got=False):
        def one(i):
            s = jnp.maximum(table[half + target, i], 0)
            j = target * capacity + i
            values = (
                encode(raw[chunk % 2][0, s]),
                raw[chunk % 2][1, s].astype(jnp.bfloat16),
                raw[chunk % 2][2, s].astype(jnp.bfloat16),
            )
            for k, value in enumerate(values):
                if to_got:
                    got[chunk][k, j] = value
                else:
                    sent[chunk, k, j] = value

        loop(0, capacity, one)

    waiting = []

    def send(copies):
        start(waiting)
        waiting[:] = copies

    for chunk in range(chunks):
        loaded(chunk).wait()
        if chunk == 0:
            for other in range(1, chunks):
                start(grad_loads(other))
            if chunks > 1:
                start(loads(1))
        split = chunk == chunks - 1 and len(cuts) > 1
        for i, target in enumerate(targets):
            pack(chunk, target)
            if chunk == 0 and i == 0:
                pl.semaphore_wait(barrier, groups - 1 + chips)
                for other in range(chunks):
                    start([twin_copy(other, k) for k in reversed(range(chips))])
            if not split:
                send([wide(chunk, 0, False, me, target)])
        if split:
            send(
                [wide(chunk, 0, False, me, targets[-1])]
                + [
                    wide(chunk, i, True, me, target)
                    for i in range(len(cuts))
                    for target in targets[:-1]
                ]
            )
        pack(chunk, me, True)
        if chunk + 2 < chunks:
            start(loads(chunk + 2))
        send([])
        for copy in grad_loads(chunk):
            copy.wait()
        for k in across:
            twin_copy(chunk, k).wait_recv()

            def join(s, chunk=chunk, k=k):
                total = own_far[chunk, k - 1, s].astype(jnp.float32) + twin_far[
                    chunk, k - 1, s
                ].astype(jnp.float32)
                own_far[chunk, k - 1, s] = total.astype(jnp.bfloat16)

            loop(0, slots, join)
            far_copy(chunk, k).start()

    def pass_on(step):
        for k in across:
            far_wait_here = spread(step, far(k), twin, relay_send.at[k], last_recv.at[step, k - 1])
            far_wait_here.wait_recv()
            relay(step, k).start()

    ready = set()
    for step, entry in enumerate(order):
        chunk, role, piece = entry
        if chunk not in ready:
            ready.add(chunk)
            twin_copy(chunk, 0).wait_recv()
            for k in across:
                far_wait(chunk, k).wait_recv()
        if role is None:
            for source in sources[1:]:
                wide(chunk, 0, False, source, me).wait_recv()
        elif role > 0:
            wide(chunk, piece, role > 1, sources[role], me).wait_recv()

        def update(source, i, chunk=chunk):
            p = jnp.maximum(table[source, i], 0)
            j = source * capacity + i
            grad = own_here[chunk][p].astype(jnp.float32) + twin_here[chunk][p].astype(jnp.float32)
            for k in across:
                grad = grad + far_here[chunk][k - 1][p].astype(jnp.float32)
            weight_here, first_here, second_here = adam_step(
                decode(got[chunk][0, j]),
                got[chunk][1, j].astype(jnp.float32),
                got[chunk][2, j].astype(jnp.float32),
                grad * (1.0 / replicas),
            )
            weights[j, band(chunk, mine)] = weight_here.astype(jnp.bfloat16)
            weight_new[j, band(chunk)] = weight_here
            first_new[j, band(chunk)] = first_here
            second_new[j, band(chunk)] = second_here

        for source, begin, size in rows_of(entry):
            loop(begin, size, functools.partial(update, source))
        start([far_spread(step, k) for k in across])
        twin_spread(step).start()
        if step >= LAG:
            pass_on(step - LAG)
    for step in range(max(len(order) - LAG, 0), len(order)):
        pass_on(step)

    whole(twin, last_send.at[0], twin_last.at[0]).wait_recv()
    whole(mine, last_send.at[0], twin_last.at[0]).wait_send()
    for k in across:
        whole(mine, last_send.at[k], twin_last.at[0]).wait_send()
        whole(far(k), relay_send.at[k], relay_recv.at[k]).wait_send()
        whole(far_twin(k), relay_send.at[k], relay_recv.at[k]).wait_recv()
        every(own_far.at[:, k - 1], far_send.at[k], far_recv.at[0, 0]).wait_send()
    for k in range(chips):
        every(twin_far.at[:, max(k - 1, 0)], twin_send.at[k], twin_recv.at[0, 0]).wait_send()
    for chunk in range(chunks):
        wide_sent(chunk).wait_send()


def place_kernel(
    groups, capacity, table, weight, first, second, weights,
    weight_new, first_new, second_new, weights_new, sem,
):
    slots = weight_new.shape[0]
    pairs = ((weight, weight_new), (first, first_new), (second, second_new), (weights, weights_new))

    def one(source, i):
        p = table[source, i]
        j = source * capacity + i

        def move():
            for k, (held, target) in enumerate(pairs):
                pltpu.make_async_copy(held.at[j], target.at[p], sem.at[k]).start()

        if groups * capacity == slots:
            move()
        else:
            pl.when(p >= 0)(move)

    for source in range(groups):
        loop(0, capacity, functools.partial(one, source))
    for k, (held, target) in enumerate(pairs):
        pltpu.make_async_copy(held.at[pl.ds(0, slots)], target, sem.at[k]).wait()


def exchange(dest_table, weight, first, second, grads, groups, replicas, capacity):
    slots, rows, lanes = weight.shape
    chunks = rows // ROWS
    chips = replicas // 2
    length = groups * capacity
    lines = 8 * pl.cdiv(groups, 8)
    wide = LANES * pl.cdiv(capacity, LANES)
    spare = -dest_table.shape[0] % LANES
    dest = jnp.pad(dest_table, (0, spare)) if spare else dest_table
    dest = dest.reshape(-1, LANES)
    anywhere = pl.BlockSpec(memory_space=pl.ANY)
    near = pl.BlockSpec(memory_space=pltpu.VMEM)
    table = pl.BlockSpec(memory_space=pltpu.SMEM)
    dma = pltpu.SemaphoreType.DMA
    cuts = len(cut_of(groups, capacity))
    steps = len(schedule(groups, chunks, cuts))
    half = jnp.bfloat16
    tile = ROWS * lanes
    scratch = (
        2 * 3 * slots * tile * 4
        + chunks * 2 * 3 * length * tile * 2
        + chunks * slots * tile * 2 * (2 + 3 * (chips - 1))
    )
    whole = pltpu.VMEM((length, rows, lanes), jnp.float32)
    *results, routed = pl.pallas_call(
        functools.partial(exchange_kernel, groups, replicas, capacity, chunks),
        out_shape=(
            whole, whole, whole,
            pltpu.VMEM((length,) + grads.shape[2:], half),
            pltpu.VMEM((2 * lines, wide), jnp.int32),
        ),
        in_specs=[anywhere] * 5,
        out_specs=(near,) * 5,
        scratch_shapes=[
            pltpu.SMEM((2 * lines, wide), jnp.int32),
            pltpu.VMEM(dest.shape, jnp.int32),
            [pltpu.VMEM((3, slots, ROWS, lanes), jnp.float32)] * 2,
            pltpu.VMEM((chunks, 3, length, ROWS, lanes), half),
            [pltpu.VMEM((3, length, ROWS, lanes), half)] * chunks,
            [pltpu.VMEM((slots, ROWS, lanes), half)] * chunks,
            pltpu.VMEM((chunks, chips - 1, slots, ROWS, lanes), half),
            [pltpu.VMEM((slots, ROWS, lanes), half)] * chunks,
            pltpu.VMEM((chunks, chips - 1, slots, ROWS, lanes), half),
            [[pltpu.VMEM((slots, ROWS, lanes), half)] * (chips - 1)] * chunks,
            dma((2,)),
            dma((2,)),
            dma((chunks, chips)),
            dma((chunks,)),
            dma((chunks + cuts - 1, groups)),
            dma((chips,)),
            dma((chunks, chips)),
            dma((chips,)),
            dma((chunks, chips)),
            dma((chips,)),
            dma((steps, chips - 1)),
            dma((1,)),
            dma((chips,)),
            dma((chips,)),
        ],
        compiler_params=pltpu.CompilerParams(
            collective_id=0, has_side_effects=True, vmem_limit_bytes=scratch + SPARE
        ),
        name="exchange",
    )(dest, weight, first, second, grads)
    shape = jax.ShapeDtypeStruct(weight.shape, jnp.float32)
    return pl.pallas_call(
        functools.partial(place_kernel, groups, capacity),
        out_shape=(shape, shape, shape, jax.ShapeDtypeStruct(grads.shape[1:], half)),
        in_specs=[table] + [anywhere] * 4,
        out_specs=(anywhere,) * 4,
        scratch_shapes=[dma((4,))],
        compiler_params=pltpu.CompilerParams(vmem_limit_bytes=SPARE),
        name="place",
    )(routed, *results)


def shards(master_weight, first_moment, second_moment, grads, dest_table):
    groups = lax.axis_size("tensor")
    slots = master_weight.shape[0]
    capacity = 2 * ((slots + 2 * groups - 1) // (2 * groups))
    replicas = lax.axis_size("dp")
    return exchange(
        dest_table, master_weight, first_moment, second_moment, grads,
        groups, replicas, capacity,
    )


def solution(mesh):
    placed = (
        P(("section", "tensor"), "dp", None),
        P(("section", "tensor"), "dp", None),
        P(("section", "tensor"), "dp", None),
        P("dp", ("section", "tensor"), None, None),
        P(),
    )
    return jax.shard_map(
        shards,
        mesh=mesh,
        in_specs=placed,
        out_specs=(
            P(("section", "tensor"), "dp", None),
            P(("section", "tensor"), "dp", None),
            P(("section", "tensor"), "dp", None),
            P(("section", "tensor"), None, None),
        ),
        check_vma=False,
    )
```

```python
import functools
import math

import jax
import jax.numpy as jnp
from jax import lax
from jax.experimental import pallas as pl
from jax.experimental.pallas import tpu as pltpu
from jax.sharding import PartitionSpec as P

STEP = 10


learn_rate = 0.04
decay_rate = 1.5
beta_first = 0.9
beta_second = 0.95
epsilon = 1e-08


def adam_step(weight, first, second, grad):
    first_new = beta_first * first + (1.0 - beta_first) * grad
    second_new = beta_second * second + (1.0 - beta_second) * grad * grad
    first_hat = first_new * (1.0 / (1.0 - beta_first**STEP))
    second_hat = second_new * (1.0 / (1.0 - beta_second**STEP))
    weight_new = weight - learn_rate * (
        first_hat / (jnp.sqrt(second_hat) + epsilon) + decay_rate * weight
    )
    return (weight_new, first_new, second_new)


ROWS = 8
SCALE = 8192.0
SPARE = 512 * 1024
LANES = 128
HELD = 4096
LINE = 4
LAG = 4
DIRECT = 2
MESH = pl.DeviceIdType.MESH


def encode(weight):
    scaled = weight * SCALE
    square = scaled * scaled
    fourth = square * square
    return (scaled * jnp.abs(scaled) * square * fourth).astype(jnp.bfloat16)


def decode(code):
    wide = code.astype(jnp.float32)
    root = jnp.sqrt(jnp.sqrt(jnp.sqrt(jnp.abs(wide)))) * (1.0 / SCALE)
    return jnp.where(wide < 0.0, -root, root)


def loop(start, size, body):
    lax.fori_loop(0, size, lambda i, carry: (body(start + i), carry)[1], 0, unroll=math.gcd(size, 8))


def rows_from(flat, groups, slots):
    width = LANES * pl.cdiv(slots, LANES)
    found = []
    for group in range(groups):
        first, extra = divmod(group * slots, LANES)
        count = pl.cdiv(extra + slots, LANES)
        row = [flat[first + i : first + i + 1] for i in range(count)]
        row = jnp.concatenate(row, axis=1) if count > 1 else row[0]
        if extra:
            row = pltpu.roll(row, count * LANES - extra, 1)
        found.append(row[:, :width])
    return found


def lines_of(groups):
    return groups if groups % 4 == 0 else 8 * pl.cdiv(groups, 8)


def routes(flat, groups, slots, capacity, me):
    rows = rows_from(flat, groups, slots)
    width = rows[0].shape[1]
    lines = lines_of(groups)
    leaving = rows[0]
    for group in range(1, groups):
        leaving = jnp.where(me == group, rows[group], leaving)
    unused = [jnp.full_like(leaving, -1)] * (lines - groups)
    table = jnp.concatenate(rows + unused + [leaving] * groups + unused, axis=0)
    lane = lax.broadcasted_iota(jnp.int32, table.shape, 1)
    line = lax.broadcasted_iota(jnp.int32, table.shape, 0)
    table = table - jnp.where(line < lines, me, line - lines) * slots
    taken = (table >= 0) & (table < slots) & (lane < slots)
    taken = taken & (jnp.where(line < lines, line, line - lines) < groups)
    before = taken.astype(jnp.int32)
    step = 1
    while step < slots:
        total = before
        for shift in range(step, min(4 * step, slots), step):
            total = total + jnp.where(lane >= shift, pltpu.roll(before, shift, 1), 0)
        before = total
        step *= 4
    held = jnp.where(line < lines, table, lane) + 1 + HELD * (lane + 1 - before)
    held = jnp.where(taken, held, 0)
    reach = slots - capacity if groups * capacity == slots else slots - 1
    step = 1
    while step <= reach:
        digit = jnp.bitwise_and(held, 3 * HELD * step)
        total = jnp.where(digit == 0, held, 0)
        for shift in range(step, min(4 * step, reach + 1), step):
            moved = jnp.where(digit == HELD * shift, held, 0)
            total = total + pltpu.roll(moved, width - shift, 1)
        held = total
        step *= 4
    return jnp.bitwise_and(held, HELD - 1) - 1


def cut_of(groups, capacity):
    if groups == LINE and capacity % 8 == 0 and capacity > 32:
        return (capacity - 32, 16, 8, 8)
    return (capacity,)


def schedule(groups, chunks, cuts):
    if groups != LINE:
        return [(chunk, None, 0) for chunk in range(chunks)]
    last = chunks - 1
    timed = []
    for chunk in range(chunks):
        timed.append((chunk + 1.6, chunk, 0, 0))
        timed.append((chunk + 2.0, chunk, 1, 0))
        for role, when in ((2, 2.3), (3, 3.7)):
            count = cuts if chunk == last and role == 3 else 1
            late = last + 10.0 * role if chunk == last else chunk * 2.0 + when
            timed += [(late + piece, chunk, role, piece) for piece in range(count)]
    return [entry[1:] for entry in sorted(timed)]


def exchange_kernel(
    groups, replicas, capacity, chunks,
    dest, weight, first, second, grads,
    weight_new, first_new, second_new, weights, table_out,
    table, flat,
    raw, sent, got, own_here, own_far, twin_here, twin_far, far_here,
    table_sem, load_sem, own_sem, wide_send, wide_recv, twin_send, twin_recv, far_send, far_recv,
    last_send, last_recv, twin_last, relay_send, relay_recv, direct_send,
):
    slots, rows = weight.shape[0], weight.shape[1]
    me = lax.axis_index("tensor")
    mine = lax.axis_index("dp")
    chips = replicas // 2
    core = lax.rem(mine, 2)
    twin = mine + 1 - 2 * core
    across = range(1, chips)
    line = groups == LINE
    cuts = cut_of(groups, capacity)
    order = schedule(groups, chunks, len(cuts))
    straight = sum(cuts[-DIRECT:]) if line and len(cuts) > DIRECT else 0
    straight = 0 if straight * ROWS % rows else straight
    relayed = len(order) - (DIRECT if straight else 0)
    if line:
        side = me // 2
        near = me + 1 - 2 * lax.rem(me, 2)
        targets = [3 - me, lax.rem(me + 2, 4), near]
        sources = [me, near, 3 - 3 * side, 2 - side]
    else:
        targets = [lax.rem(me + k, groups) for k in range(1, groups)]
        sources = [lax.rem(me + groups - k, groups) for k in range(groups)]

    def far(k):
        return lax.rem(mine + 2 * k, replicas)

    def far_twin(k):
        return lax.rem(mine + 2 * k, replicas) + 1 - 2 * core

    def band(chunk, owner=None):
        if owner is None:
            return pl.ds(chunk * ROWS, ROWS)
        return pl.ds(pl.multiple_of(owner * rows + chunk * ROWS, ROWS), ROWS)

    def loads(chunk):
        return [
            pltpu.make_async_copy(
                ref.at[:, band(chunk), :],
                raw[chunk % 2][k],
                load_sem.at[chunk % 2, k],
            )
            for k, ref in enumerate((weight, first, second))
        ]

    def cut(chunk, piece, split):
        if chunk == chunks - 1 and split:
            return sum(cuts[:piece]), cuts[piece]
        return 0, capacity

    def slot(chunk, role, piece):
        last = chunks - 1
        return 3 * chunk + role - 1 + (piece if role == 3 and chunk == last else 0)

    def slot_there(chunk, piece, target):
        if not line:
            return chunk * groups + me
        if target is near:
            return slot(chunk, 1, 0)
        inner = lax.rem((me + 1) // 2, 2)
        return slot(chunk, 2, 0) + inner * (1 + piece)

    def slot_here(chunk, role, piece, source):
        return slot(chunk, role, piece) if line else chunk * groups + source

    def wide(chunk, piece, split, source, target, place=0, kinds=slice(None)):
        begin, size = cut(chunk, piece, split)
        return pltpu.make_async_remote_copy(
            src_ref=sent.at[chunk, kinds, pl.ds(target * capacity + begin, size)],
            dst_ref=got[chunk].at[kinds, pl.ds(source * capacity + begin, size)],
            send_sem=wide_send.at[0],
            recv_sem=wide_recv.at[place],
            device_id={"tensor": target},
            device_id_type=MESH,
        )

    def own_far_load(chunk, k):
        return pltpu.make_async_copy(
            grads.at[0, :, band(chunk, far(k)), :],
            own_far.at[chunk, k - 1],
            own_sem.at[1 + chunk * (chips - 1) + k - 1],
        )

    def own_here_load(chunk):
        return pltpu.make_async_copy(
            grads.at[0, :, band(chunk, mine), :], own_here[chunk], own_sem.at[0]
        )

    def grad_loads(chunk):
        return [own_far_load(chunk, k) for k in across] + [own_here_load(chunk)]

    def twin_copy(chunk, k):
        return pltpu.make_async_remote_copy(
            src_ref=grads.at[0, :, band(chunk, far_twin(k)), :],
            dst_ref=twin_far.at[chunk, k - 1] if k else twin_here[chunk],
            send_sem=twin_send.at[k],
            recv_sem=twin_recv.at[1 + chunk * (chips - 1) + k - 1 if k else 0],
            device_id={"dp": twin},
            device_id_type=MESH,
        )

    def far_copy(chunk, k):
        return pltpu.make_async_remote_copy(
            src_ref=own_far.at[chunk, k - 1],
            dst_ref=far_here[chunk][chips - k - 1],
            send_sem=far_send.at[k - 1],
            recv_sem=far_recv.at[chunk, chips - k - 1],
            device_id={"dp": far(k)},
            device_id_type=MESH,
        )

    def far_wait(chunk, k):
        return pltpu.make_async_remote_copy(
            src_ref=own_far.at[chunk, chips - k - 1],
            dst_ref=far_here[chunk][k - 1],
            send_sem=far_send.at[chips - k - 1],
            recv_sem=far_recv.at[chunk, k - 1],
            device_id={"dp": far(k)},
            device_id_type=MESH,
        )

    def extent(entry):
        chunk, role, piece = entry
        if role is None:
            return 0, groups * capacity
        begin, size = cut(chunk, piece, role > 2)
        return sources[role] * capacity + begin, size

    def rows_of(entry):
        if entry[1] is None:
            return [(source, 0, capacity) for source in range(groups)]
        return [(sources[entry[1]], *cut(entry[0], entry[2], entry[1] > 2))]

    def spread(step, owner, target, send, recv):
        start, size = extent(order[step])
        here = weights.at[pl.ds(start, size), band(order[step][0], owner), :]
        return pltpu.make_async_remote_copy(
            src_ref=here,
            dst_ref=here,
            send_sem=send,
            recv_sem=recv,
            device_id={"dp": target},
            device_id_type=MESH,
        )

    def far_spread(step, k):
        return spread(step, mine, far(k), last_send.at[k], last_recv.at[step, chips - k - 1])

    def twin_spread(step):
        return spread(step, mine, twin, last_send.at[0], twin_last.at[0])

    def relay(step, k):
        return spread(step, far(k), twin, relay_send.at[k - 1], relay_recv.at[k - 1])

    def direct_spread(step, k):
        return spread(step, mine, far_twin(k), direct_send.at[k - 1], relay_recv.at[chips - k - 1])

    def whole(owner, send, recv):
        here = weights.at[:, pl.ds(pl.multiple_of(owner * rows, ROWS), rows), :]
        return pltpu.make_async_remote_copy(
            src_ref=here,
            dst_ref=here,
            send_sem=send,
            recv_sem=recv,
            device_id={"dp": twin},
            device_id_type=MESH,
        )

    def every(ref, send, recv):
        return pltpu.make_async_remote_copy(
            src_ref=ref, dst_ref=ref, send_sem=send, recv_sem=recv,
            device_id={"dp": twin}, device_id_type=MESH,
        )

    def start(copies):
        for copy in copies:
            copy.start()

    fetch = pltpu.make_async_copy(dest, flat, table_sem.at[0])
    fetch.start()
    barrier = pltpu.get_barrier_semaphore()
    for target in targets:
        pl.semaphore_signal(barrier, inc=1, device_id={"tensor": target}, device_id_type=MESH)
    pl.semaphore_signal(barrier, inc=1, device_id={"dp": twin}, device_id_type=MESH)
    for k in across:
        pl.semaphore_signal(barrier, inc=1, device_id={"dp": far(k)}, device_id_type=MESH)
    half = table_out.shape[0] // 2
    fetch.wait()
    start(loads(0))
    table_out[...] = routes(flat[...], groups, slots, capacity, me)[:, : table_out.shape[1]]
    copy = pltpu.make_async_copy(table_out, table, table_sem.at[1])
    copy.start()
    copy.wait()

    def pack(chunk, target, to_got=False, kinds=range(3)):
        def one(i):
            s = jnp.maximum(table[half + target, i], 0)
            j = target * capacity + i
            for k in kinds:
                value = raw[chunk % 2][k][s]
                value = encode(value) if k == 0 else value.astype(jnp.bfloat16)
                if to_got:
                    got[chunk][k, j] = value
                else:
                    sent[chunk, k, j] = value

        loop(0, capacity, one)

    waiting = []

    def send(copies):
        start(waiting)
        waiting[:] = copies

    for chunk in range(chunks):
        if chunk:
            for load in loads(chunk):
                load.wait()
        split = chunk == chunks - 1 and len(cuts) > 1
        for i, target in enumerate(targets):
            if chunk == 0 and i == 0:
                for k, load in enumerate(loads(0)):
                    load.wait()
                    pack(0, target, kinds=(k,))
                    if k == 0:
                        pl.semaphore_wait(barrier, groups - 1 + chips)
                        start([twin_copy(0, i) for i in reversed(range(chips))])
                    if not split:
                        send([
                            wide(0, 0, False, me, target, slot_there(0, 0, target), pl.ds(k, 1))
                        ])
                        if k == 0:
                            send([])
                for other in range(chunks):
                    start(grad_loads(other))
                if chunks > 1:
                    start(loads(1))
                for other in range(1, chunks):
                    start([twin_copy(other, k) for k in reversed(range(chips))])
                continue
            pack(chunk, target)
            if not split:
                send([wide(chunk, 0, False, me, target, slot_there(chunk, 0, target))])
        if split:
            send(
                [wide(chunk, 0, False, me, targets[-1], slot_there(chunk, 0, targets[-1]))]
                + [
                    wide(chunk, i, True, me, target, slot_there(chunk, i, target))
                    for i in range(len(cuts))
                    for target in targets[:-1]
                ]
            )
        pack(chunk, me, True)
        if chunk + 2 < chunks:
            start(loads(chunk + 2))
        send([])
        for k in across:
            own_far_load(chunk, k).wait()
            twin_copy(chunk, k).wait_recv()

            def join(s, chunk=chunk, k=k):
                total = own_far[chunk, k - 1, s].astype(jnp.float32) + twin_far[
                    chunk, k - 1, s
                ].astype(jnp.float32)
                own_far[chunk, k - 1, s] = total.astype(jnp.bfloat16)

            loop(0, slots, join)
            far_copy(chunk, k).start()

    def far_got(step, k):
        return spread(step, far(k), twin, relay_send.at[k - 1], last_recv.at[step, k - 1])

    def pass_on(step):
        for k in across:
            far_got(step, k).wait_recv()
            relay(step, k).start()

    pltpu.make_async_copy(own_far.at[:, 0], own_far.at[:, 0], own_sem.at[0]).wait()
    every(twin_far.at[:, 0], twin_send.at[0], twin_recv.at[0]).wait_recv()
    ready = set()
    behind = []
    for step, entry in enumerate(order):
        chunk, role, piece = entry
        if chunk not in ready:
            ready.add(chunk)
            for k in across:
                far_wait(chunk, k).wait_recv()
        if role is None:
            for source in sources[1:]:
                wide(chunk, 0, False, source, me, slot_here(chunk, 0, 0, source)).wait_recv()
        elif role > 0:
            place = slot_here(chunk, role, piece, sources[role])
            wide(chunk, piece, role > 2, sources[role], me, place).wait_recv()

        def update(source, i, chunk=chunk):
            p = jnp.maximum(table[source, i], 0)
            j = source * capacity + i
            grad = own_here[chunk][p].astype(jnp.float32) + twin_here[chunk][p].astype(jnp.float32)
            for k in across:
                grad = grad + far_here[chunk][k - 1][p].astype(jnp.float32)
            weight_here, first_here, second_here = adam_step(
                decode(got[chunk][0, j]),
                got[chunk][1, j].astype(jnp.float32),
                got[chunk][2, j].astype(jnp.float32),
                grad * (1.0 / replicas),
            )
            weights[j, band(chunk, mine)] = weight_here.astype(jnp.bfloat16)
            weight_new[j, band(chunk)] = weight_here
            first_new[j, band(chunk)] = first_here
            second_new[j, band(chunk)] = second_here

        for source, begin, size in rows_of(entry):
            loop(begin, size, functools.partial(update, source))
        start([far_spread(step, k) for k in across])
        if step >= relayed:
            start([direct_spread(step, k) for k in across])
        else:
            behind.append(step)
        twin_spread(step).start()
        while len(behind) > (LAG if chunk < chunks - 1 else 2) or (behind and step >= relayed):
            pass_on(behind.pop(0))
    for step in behind:
        pass_on(step)
    for step in range(relayed, len(order)):
        for k in across:
            far_got(step, k).wait_recv()

    whole(twin, last_send.at[0], twin_last.at[0]).wait_recv()
    for k in across:
        whole(far_twin(k), relay_send.at[k - 1], relay_recv.at[k - 1]).wait_recv()
    whole(mine, last_send.at[0], twin_last.at[0]).wait_send()
    for k in across:
        whole(mine, last_send.at[k], twin_last.at[0]).wait_send()
        passed = weights.at[pl.ds(0, groups * capacity - straight * ROWS // rows), pl.ds(0, rows)]
        every(passed, relay_send.at[k - 1], twin_last.at[0]).wait_send()
        if straight:
            passed = weights.at[pl.ds(0, straight), pl.ds(0, ROWS)]
            every(passed, direct_send.at[k - 1], twin_last.at[0]).wait_send()
        every(own_far.at[:, k - 1], far_send.at[k - 1], twin_last.at[0]).wait_send()
    for k in range(chips):
        every(twin_far.at[:, max(k - 1, 0)], twin_send.at[k], twin_last.at[0]).wait_send()
    gone = sent.at[:, :, pl.ds(0, (groups - 1) * capacity)]
    every(gone, wide_send.at[0], twin_last.at[0]).wait_send()


def place_kernel(
    groups, capacity, table, weight, first, second, weights,
    weight_new, first_new, second_new, weights_new, sem,
):
    slots = weight_new.shape[0]
    pairs = ((weight, weight_new), (first, first_new), (second, second_new), (weights, weights_new))

    def one(source, i):
        p = table[source, i]
        j = source * capacity + i

        def move():
            for k, (held, target) in enumerate(pairs):
                pltpu.make_async_copy(held.at[j], target.at[p], sem.at[k]).start()

        if groups * capacity == slots:
            move()
        else:
            pl.when(p >= 0)(move)

    for source in range(groups):
        loop(0, capacity, functools.partial(one, source))
    for k, (held, target) in enumerate(pairs):
        pltpu.make_async_copy(held.at[pl.ds(0, slots)], target, sem.at[k]).wait()


def exchange(dest_table, weight, first, second, grads, groups, replicas, capacity):
    slots, rows, lanes = weight.shape
    chunks = rows // ROWS
    chips = replicas // 2
    length = groups * capacity
    lines = lines_of(groups)
    wide = LANES * pl.cdiv(capacity, LANES)
    spare = -dest_table.shape[0] % LANES
    dest = jnp.pad(dest_table, (0, spare)) if spare else dest_table
    dest = dest.reshape(-1, LANES)
    anywhere = pl.BlockSpec(memory_space=pl.ANY)
    near = pl.BlockSpec(memory_space=pltpu.VMEM)
    table = pl.BlockSpec(memory_space=pltpu.SMEM)
    dma = pltpu.SemaphoreType.DMA
    cuts = len(cut_of(groups, capacity))
    steps = len(schedule(groups, chunks, cuts))
    half = jnp.bfloat16
    tile = ROWS * lanes
    scratch = (
        2 * 3 * slots * tile * 4
        + chunks * 2 * 3 * length * tile * 2
        + chunks * slots * tile * 2 * (2 + 3 * (chips - 1))
    )
    whole = pltpu.VMEM((length, rows, lanes), jnp.float32)
    *results, routed = pl.pallas_call(
        functools.partial(exchange_kernel, groups, replicas, capacity, chunks),
        out_shape=(
            whole, whole, whole,
            pltpu.VMEM((length,) + grads.shape[2:], half),
            pltpu.VMEM((2 * lines, wide), jnp.int32),
        ),
        in_specs=[anywhere] * 5,
        out_specs=(near,) * 5,
        scratch_shapes=[
            pltpu.SMEM((2 * lines, wide), jnp.int32),
            pltpu.VMEM(dest.shape, jnp.int32),
            [[pltpu.VMEM((slots, ROWS, lanes), jnp.float32)] * 3] * 2,
            pltpu.VMEM((chunks, 3, length, ROWS, lanes), half),
            [pltpu.VMEM((3, length, ROWS, lanes), half)] * chunks,
            [pltpu.VMEM((slots, ROWS, lanes), half)] * chunks,
            pltpu.VMEM((chunks, chips - 1, slots, ROWS, lanes), half),
            [pltpu.VMEM((slots, ROWS, lanes), half)] * chunks,
            pltpu.VMEM((chunks, chips - 1, slots, ROWS, lanes), half),
            [[pltpu.VMEM((slots, ROWS, lanes), half)] * (chips - 1)] * chunks,
            dma((2,)),
            dma((2, 3)),
            dma((1 + chunks * (chips - 1),)),
            dma((1,)),
            dma((3 * chunks + cuts - 1 if groups == LINE else chunks * groups,)),
            dma((chips,)),
            dma((1 + chunks * (chips - 1),)),
            dma((chips - 1,)),
            dma((chunks, chips - 1)),
            dma((chips,)),
            dma((steps, chips - 1)),
            dma((1,)),
            dma((chips - 1,)),
            dma((chips - 1,)),
            dma((chips - 1,)),
        ],
        compiler_params=pltpu.CompilerParams(
            collective_id=0, has_side_effects=True, vmem_limit_bytes=scratch + SPARE
        ),
        name="exchange",
    )(dest, weight, first, second, grads)
    shape = jax.ShapeDtypeStruct(weight.shape, jnp.float32)
    return pl.pallas_call(
        functools.partial(place_kernel, groups, capacity),
        out_shape=(shape, shape, shape, jax.ShapeDtypeStruct(grads.shape[1:], half)),
        in_specs=[table] + [anywhere] * 4,
        out_specs=(anywhere,) * 4,
        scratch_shapes=[dma((4,))],
        compiler_params=pltpu.CompilerParams(vmem_limit_bytes=SPARE),
        name="place",
    )(routed, *results)


def shards(master_weight, first_moment, second_moment, grads, dest_table):
    groups = lax.axis_size("tensor")
    slots = master_weight.shape[0]
    capacity = 2 * ((slots + 2 * groups - 1) // (2 * groups))
    replicas = lax.axis_size("dp")
    return exchange(
        dest_table, master_weight, first_moment, second_moment, grads,
        groups, replicas, capacity,
    )


def solution(mesh):
    placed = (
        P(("section", "tensor"), "dp", None),
        P(("section", "tensor"), "dp", None),
        P(("section", "tensor"), "dp", None),
        P("dp", ("section", "tensor"), None, None),
        P(),
    )
    return jax.shard_map(
        shards,
        mesh=mesh,
        in_specs=placed,
        out_specs=(
            P(("section", "tensor"), "dp", None),
            P(("section", "tensor"), "dp", None),
            P(("section", "tensor"), "dp", None),
            P(("section", "tensor"), None, None),
        ),
        check_vma=False,
    )
```

```python
import functools
import math

import jax
import jax.numpy as jnp
from jax import lax
from jax.experimental import pallas as pl
from jax.experimental.pallas import tpu as pltpu
from jax.sharding import PartitionSpec as P

STEP = 10


learn_rate = 0.04
decay_rate = 1.5
beta_first = 0.9
beta_second = 0.95
epsilon = 1e-08


def adam_step(weight, first, second, grad):
    first_new = beta_first * first + (1.0 - beta_first) * grad
    second_new = beta_second * second + (1.0 - beta_second) * grad * grad
    first_hat = first_new * (1.0 / (1.0 - beta_first**STEP))
    second_hat = second_new * (1.0 / (1.0 - beta_second**STEP))
    weight_new = weight - learn_rate * (
        first_hat / (jnp.sqrt(second_hat) + epsilon) + decay_rate * weight
    )
    return (weight_new, first_new, second_new)


ROWS = 8
SCALE = 8192.0
SPARE = 512 * 1024
LANES = 128
HELD = 4096
LINE = 4
LAG = 4
DIRECT = 2
SHARES = 4
MESH = pl.DeviceIdType.MESH


def encode(weight):
    scaled = weight * SCALE
    square = scaled * scaled
    fourth = square * square
    return (scaled * jnp.abs(scaled) * square * fourth).astype(jnp.bfloat16)


def decode(code):
    wide = code.astype(jnp.float32)
    root = jnp.sqrt(jnp.sqrt(jnp.sqrt(jnp.abs(wide)))) * (1.0 / SCALE)
    return jnp.where(wide < 0.0, -root, root)


def loop(start, size, body):
    lax.fori_loop(0, size, lambda i, carry: (body(start + i), carry)[1], 0, unroll=math.gcd(size, 8))


def rows_from(flat, groups, slots):
    width = LANES * pl.cdiv(slots, LANES)
    found = []
    for group in range(groups):
        first, extra = divmod(group * slots, LANES)
        count = pl.cdiv(extra + slots, LANES)
        row = [flat[first + i : first + i + 1] for i in range(count)]
        row = jnp.concatenate(row, axis=1) if count > 1 else row[0]
        if extra:
            row = pltpu.roll(row, count * LANES - extra, 1)
        found.append(row[:, :width])
    return found


def lines_of(groups):
    return groups if groups % 4 == 0 else 8 * pl.cdiv(groups, 8)


def routes(flat, groups, slots, capacity, me):
    rows = rows_from(flat, groups, slots)
    width = rows[0].shape[1]
    lines = lines_of(groups)
    leaving = rows[0]
    for group in range(1, groups):
        leaving = jnp.where(me == group, rows[group], leaving)
    unused = [jnp.full_like(leaving, -1)] * (lines - groups)
    table = jnp.concatenate(rows + unused + [leaving] * groups + unused, axis=0)
    lane = lax.broadcasted_iota(jnp.int32, table.shape, 1)
    line = lax.broadcasted_iota(jnp.int32, table.shape, 0)
    table = table - jnp.where(line < lines, me, line - lines) * slots
    taken = (table >= 0) & (table < slots) & (lane < slots)
    taken = taken & (jnp.where(line < lines, line, line - lines) < groups)
    before = taken.astype(jnp.int32)
    step = 1
    while step < slots:
        total = before
        for shift in range(step, min(4 * step, slots), step):
            total = total + jnp.where(lane >= shift, pltpu.roll(before, shift, 1), 0)
        before = total
        step *= 4
    held = jnp.where(line < lines, table, lane) + 1 + HELD * (lane + 1 - before)
    held = jnp.where(taken, held, 0)
    reach = slots - capacity if groups * capacity == slots else slots - 1
    step = 1
    while step <= reach:
        digit = jnp.bitwise_and(held, 3 * HELD * step)
        total = jnp.where(digit == 0, held, 0)
        for shift in range(step, min(4 * step, reach + 1), step):
            moved = jnp.where(digit == HELD * shift, held, 0)
            total = total + pltpu.roll(moved, width - shift, 1)
        held = total
        step *= 4
    return jnp.bitwise_and(held, HELD - 1) - 1


def cut_of(groups, capacity):
    if groups == LINE and capacity % 8 == 0 and capacity > 32:
        return (capacity - 32, 16, 8, 8)
    return (capacity,)


def schedule(groups, chunks, cuts):
    if groups != LINE:
        return [(chunk, None, 0) for chunk in range(chunks)]
    last = chunks - 1
    timed = []
    for chunk in range(chunks):
        timed.append((chunk + 1.6, chunk, 0, 0))
        timed.append((chunk + 2.0, chunk, 1, 0))
        for role, when in ((2, 2.3), (3, 3.7)):
            count = cuts if chunk == last and role == 3 else 1
            late = last + 10.0 * role if chunk == last else chunk * 2.0 + when
            timed += [(late + piece, chunk, role, piece) for piece in range(count)]
    return [entry[1:] for entry in sorted(timed)]


def exchange_kernel(
    groups, replicas, capacity, chunks,
    dest, weight, first, second, grads,
    weight_new, first_new, second_new, weights, table,
    table_out, flat,
    raw, sent, got, own_here, own_far, twin_here, twin_far, far_here,
    table_sem, load_sem, own_sem, wide_send, wide_recv, twin_send, twin_recv, far_send, far_recv,
    last_send, last_recv, twin_last, relay_send, relay_recv, direct_send,
):
    slots, rows = weight.shape[0], weight.shape[1]
    me = lax.axis_index("tensor")
    mine = lax.axis_index("dp")
    chips = replicas // 2
    core = lax.rem(mine, 2)
    twin = mine + 1 - 2 * core
    across = range(1, chips)
    line = groups == LINE
    cuts = cut_of(groups, capacity)
    order = schedule(groups, chunks, len(cuts))
    straight = sum(cuts[-DIRECT:]) if line and len(cuts) > DIRECT else 0
    straight = 0 if straight * ROWS % rows else straight
    relayed = len(order) - (DIRECT if straight else 0)
    if line:
        side = me // 2
        near = me + 1 - 2 * lax.rem(me, 2)
        inner = lax.rem((me + 1) // 2, 2)
        opposite, facing = lax.rem(me + 2, 4), 3 - me
        first_target = inner * opposite + (1 - inner) * facing
        targets = [first_target, opposite + facing - first_target, near]
        sources = [me, near, 3 - 3 * side, 2 - side]
    else:
        targets = [lax.rem(me + k, groups) for k in range(1, groups)]
        sources = [lax.rem(me + groups - k, groups) for k in range(groups)]

    def far(k):
        return lax.rem(mine + 2 * k, replicas)

    def far_twin(k):
        return lax.rem(mine + 2 * k, replicas) + 1 - 2 * core

    def band(chunk, owner=None):
        if owner is None:
            return pl.ds(chunk * ROWS, ROWS)
        return pl.ds(pl.multiple_of(owner * rows + chunk * ROWS, ROWS), ROWS)

    def loads(chunk, kinds=range(3)):
        share = slots // SHARES if chunk == 0 and slots % SHARES == 0 else slots
        return [
            pltpu.make_async_copy(
                (weight, first, second)[k].at[pl.ds(begin, share), band(chunk), :],
                raw[chunk % 2][k].at[pl.ds(begin, share)],
                load_sem.at[chunk % 2, k],
            )
            for k in kinds
            for begin in range(0, slots, share)
        ]

    def loaded(chunk, k):
        pltpu.make_async_copy(raw[chunk % 2][k], raw[chunk % 2][k], load_sem.at[chunk % 2, k]).wait()

    def cut(chunk, piece, split):
        if chunk == chunks - 1 and split:
            return sum(cuts[:piece]), cuts[piece]
        return 0, capacity

    def slot(chunk, role, piece):
        last = chunks - 1
        return 3 * chunk + role - 1 + (piece if role == 3 and chunk == last else 0)

    def slot_there(chunk, piece, target):
        if not line:
            return chunk * groups + me
        if target is near:
            return slot(chunk, 1, 0)
        return slot(chunk, 2, 0) + inner * (1 + piece)

    def slot_here(chunk, role, piece, source):
        return slot(chunk, role, piece) if line else chunk * groups + source

    def wide(chunk, piece, split, source, target, place=0, kinds=slice(None)):
        begin, size = cut(chunk, piece, split)
        return pltpu.make_async_remote_copy(
            src_ref=sent.at[chunk, kinds, pl.ds(target * capacity + begin, size)],
            dst_ref=got[chunk].at[kinds, pl.ds(source * capacity + begin, size)],
            send_sem=wide_send.at[0],
            recv_sem=wide_recv.at[place],
            device_id={"tensor": target},
            device_id_type=MESH,
        )

    def own_far_load(chunk, k):
        return pltpu.make_async_copy(
            grads.at[0, :, band(chunk, far(k)), :],
            own_far.at[chunk, k - 1],
            own_sem.at[1 + chunk * (chips - 1) + k - 1],
        )

    def own_here_load(chunk):
        return pltpu.make_async_copy(
            grads.at[0, :, band(chunk, mine), :], own_here[chunk], own_sem.at[0]
        )

    def grad_loads(chunk):
        return [own_far_load(chunk, k) for k in across] + [own_here_load(chunk)]

    def twin_copy(chunk, k):
        return pltpu.make_async_remote_copy(
            src_ref=grads.at[0, :, band(chunk, far_twin(k)), :],
            dst_ref=twin_far.at[chunk, k - 1] if k else twin_here[chunk],
            send_sem=twin_send.at[k],
            recv_sem=twin_recv.at[1 + chunk * (chips - 1) + k - 1 if k else 0],
            device_id={"dp": twin},
            device_id_type=MESH,
        )

    def far_copy(chunk, k):
        return pltpu.make_async_remote_copy(
            src_ref=own_far.at[chunk, k - 1],
            dst_ref=far_here[chunk][chips - k - 1],
            send_sem=far_send.at[k - 1],
            recv_sem=far_recv.at[chunk, chips - k - 1],
            device_id={"dp": far(k)},
            device_id_type=MESH,
        )

    def far_wait(chunk, k):
        return pltpu.make_async_remote_copy(
            src_ref=own_far.at[chunk, chips - k - 1],
            dst_ref=far_here[chunk][k - 1],
            send_sem=far_send.at[chips - k - 1],
            recv_sem=far_recv.at[chunk, k - 1],
            device_id={"dp": far(k)},
            device_id_type=MESH,
        )

    def extent(entry):
        chunk, role, piece = entry
        if role is None:
            return 0, groups * capacity
        begin, size = cut(chunk, piece, role > 2)
        return sources[role] * capacity + begin, size

    def rows_of(entry):
        if entry[1] is None:
            return [(source, 0, capacity) for source in range(groups)]
        return [(sources[entry[1]], *cut(entry[0], entry[2], entry[1] > 2))]

    def spread(step, owner, target, send, recv):
        start, size = extent(order[step])
        here = weights.at[pl.ds(start, size), band(order[step][0], owner), :]
        return pltpu.make_async_remote_copy(
            src_ref=here,
            dst_ref=here,
            send_sem=send,
            recv_sem=recv,
            device_id={"dp": target},
            device_id_type=MESH,
        )

    def far_spread(step, k):
        return spread(step, mine, far(k), last_send.at[k], last_recv.at[step, chips - k - 1])

    def twin_spread(step):
        return spread(step, mine, twin, last_send.at[0], twin_last.at[0])

    def relay(step, k):
        return spread(step, far(k), twin, relay_send.at[k - 1], relay_recv.at[k - 1])

    def direct_spread(step, k):
        return spread(step, mine, far_twin(k), direct_send.at[k - 1], relay_recv.at[chips - k - 1])

    def whole(owner, send, recv):
        here = weights.at[:, pl.ds(pl.multiple_of(owner * rows, ROWS), rows), :]
        return pltpu.make_async_remote_copy(
            src_ref=here,
            dst_ref=here,
            send_sem=send,
            recv_sem=recv,
            device_id={"dp": twin},
            device_id_type=MESH,
        )

    def every(ref, send, recv):
        return pltpu.make_async_remote_copy(
            src_ref=ref, dst_ref=ref, send_sem=send, recv_sem=recv,
            device_id={"dp": twin}, device_id_type=MESH,
        )

    def start(copies):
        for copy in copies:
            copy.start()

    fetch = pltpu.make_async_copy(dest, flat, table_sem.at[0])
    fetch.start()
    barrier = pltpu.get_barrier_semaphore()
    for target in targets:
        pl.semaphore_signal(barrier, inc=1, device_id={"tensor": target}, device_id_type=MESH)
    pl.semaphore_signal(barrier, inc=1, device_id={"dp": twin}, device_id_type=MESH)
    for k in across:
        pl.semaphore_signal(barrier, inc=1, device_id={"dp": far(k)}, device_id_type=MESH)
    half = table_out.shape[0] // 2
    start(loads(0, [0]))
    fetch.wait()
    table_out[...] = routes(flat[...], groups, slots, capacity, me)[:, : table_out.shape[1]]
    copy = pltpu.make_async_copy(table_out, table, table_sem.at[1])
    copy.start()
    copy.wait()
    loaded(0, 0)
    start(loads(0, [1, 2]))

    def pack(chunk, target, to_got=False, kinds=range(3)):
        def one(i):
            s = jnp.maximum(table[half + target, i], 0)
            j = target * capacity + i
            for k in kinds:
                value = raw[chunk % 2][k][s]
                value = encode(value) if k == 0 else value.astype(jnp.bfloat16)
                if to_got:
                    got[chunk][k, j] = value
                else:
                    sent[chunk, k, j] = value

        loop(0, capacity, one)

    waiting = []

    def send(copies):
        start(waiting)
        waiting[:] = copies

    for chunk in range(chunks):
        if chunk:
            for k in range(3):
                loaded(chunk, k)
        split = chunk == chunks - 1 and len(cuts) > 1
        for i, target in enumerate(targets):
            if chunk == 0 and i == 0:
                for k in range(3):
                    if k:
                        loaded(0, k)
                    pack(0, target, kinds=(k,))
                    if k == 0:
                        pl.semaphore_wait(barrier, groups - 1 + chips)
                        start([twin_copy(0, i) for i in reversed(range(chips))])
                    if not split:
                        send([
                            wide(0, 0, False, me, target, slot_there(0, 0, target), pl.ds(k, 1))
                        ])
                        if k == 0:
                            send([])
                for other in range(chunks):
                    start(grad_loads(other))
                if chunks > 1:
                    start(loads(1))
                for other in range(1, chunks):
                    start([twin_copy(other, k) for k in reversed(range(chips))])
                continue
            pack(chunk, target)
            if not split:
                send([wide(chunk, 0, False, me, target, slot_there(chunk, 0, target))])
        if split:
            send(
                [wide(chunk, 0, False, me, targets[-1], slot_there(chunk, 0, targets[-1]))]
                + [
                    wide(chunk, i, True, me, target, slot_there(chunk, i, target))
                    for i in range(len(cuts))
                    for target in targets[:-1]
                ]
            )
        pack(chunk, me, True)
        if chunk + 2 < chunks:
            start(loads(chunk + 2))
        send([])
        for k in across:
            own_far_load(chunk, k).wait()
            twin_copy(chunk, k).wait_recv()

            def join(s, chunk=chunk, k=k):
                total = own_far[chunk, k - 1, s].astype(jnp.float32) + twin_far[
                    chunk, k - 1, s
                ].astype(jnp.float32)
                own_far[chunk, k - 1, s] = total.astype(jnp.bfloat16)

            loop(0, slots, join)
            far_copy(chunk, k).start()

    def far_got(step, k):
        return spread(step, far(k), twin, relay_send.at[k - 1], last_recv.at[step, k - 1])

    def pass_on(step):
        for k in across:
            far_got(step, k).wait_recv()
            relay(step, k).start()

    pltpu.make_async_copy(own_far.at[:, 0], own_far.at[:, 0], own_sem.at[0]).wait()
    every(twin_far.at[:, 0], twin_send.at[0], twin_recv.at[0]).wait_recv()
    ready = set()
    behind = []
    for step, entry in enumerate(order):
        chunk, role, piece = entry
        if chunk not in ready:
            ready.add(chunk)
            for k in across:
                far_wait(chunk, k).wait_recv()
        if role is None:
            for source in sources[1:]:
                wide(chunk, 0, False, source, me, slot_here(chunk, 0, 0, source)).wait_recv()
        elif role > 0:
            place = slot_here(chunk, role, piece, sources[role])
            wide(chunk, piece, role > 2, sources[role], me, place).wait_recv()

        def update(source, i, chunk=chunk):
            p = jnp.maximum(table[source, i], 0)
            j = source * capacity + i
            grad = own_here[chunk][p].astype(jnp.float32) + twin_here[chunk][p].astype(jnp.float32)
            for k in across:
                grad = grad + far_here[chunk][k - 1][p].astype(jnp.float32)
            weight_here, first_here, second_here = adam_step(
                decode(got[chunk][0, j]),
                got[chunk][1, j].astype(jnp.float32),
                got[chunk][2, j].astype(jnp.float32),
                grad * (1.0 / replicas),
            )
            weights[j, band(chunk, mine)] = weight_here.astype(jnp.bfloat16)
            weight_new[j, band(chunk)] = weight_here
            first_new[j, band(chunk)] = first_here
            second_new[j, band(chunk)] = second_here

        for source, begin, size in rows_of(entry):
            loop(begin, size, functools.partial(update, source))
        start([far_spread(step, k) for k in across])
        if step >= relayed:
            start([direct_spread(step, k) for k in across])
        else:
            behind.append(step)
        twin_spread(step).start()
        while len(behind) > (LAG if chunk < chunks - 1 else 2) or (behind and step >= relayed):
            pass_on(behind.pop(0))
    for step in behind:
        pass_on(step)
    for step in range(relayed, len(order)):
        for k in across:
            far_got(step, k).wait_recv()

    whole(twin, last_send.at[0], twin_last.at[0]).wait_recv()
    for k in across:
        whole(far_twin(k), relay_send.at[k - 1], relay_recv.at[k - 1]).wait_recv()
    whole(mine, last_send.at[0], twin_last.at[0]).wait_send()
    for k in across:
        whole(mine, last_send.at[k], twin_last.at[0]).wait_send()
        passed = weights.at[pl.ds(0, groups * capacity - straight * ROWS // rows), pl.ds(0, rows)]
        every(passed, relay_send.at[k - 1], twin_last.at[0]).wait_send()
        if straight:
            passed = weights.at[pl.ds(0, straight), pl.ds(0, ROWS)]
            every(passed, direct_send.at[k - 1], twin_last.at[0]).wait_send()
        every(own_far.at[:, k - 1], far_send.at[k - 1], twin_last.at[0]).wait_send()
    for k in range(chips):
        every(twin_far.at[:, max(k - 1, 0)], twin_send.at[k], twin_last.at[0]).wait_send()
    gone = sent.at[:, :, pl.ds(0, (groups - 1) * capacity)]
    every(gone, wide_send.at[0], twin_last.at[0]).wait_send()


def place_kernel(
    groups, capacity, table, weight, first, second, weights,
    weight_new, first_new, second_new, weights_new, sem,
):
    slots = weight_new.shape[0]
    pairs = ((weight, weight_new), (first, first_new), (second, second_new), (weights, weights_new))

    def one(source, i):
        p = table[source, i]
        j = source * capacity + i

        def move():
            for k, (held, target) in enumerate(pairs):
                pltpu.make_async_copy(held.at[j], target.at[p], sem.at[k]).start()

        if groups * capacity == slots:
            move()
        else:
            pl.when(p >= 0)(move)

    for source in range(groups):
        loop(0, capacity, functools.partial(one, source))
    for k, (held, target) in enumerate(pairs):
        pltpu.make_async_copy(held.at[pl.ds(0, slots)], target, sem.at[k]).wait()


def exchange(dest_table, weight, first, second, grads, groups, replicas, capacity):
    slots, rows, lanes = weight.shape
    chunks = rows // ROWS
    chips = replicas // 2
    length = groups * capacity
    lines = lines_of(groups)
    wide = LANES * pl.cdiv(capacity, LANES)
    spare = -dest_table.shape[0] % LANES
    dest = jnp.pad(dest_table, (0, spare)) if spare else dest_table
    dest = dest.reshape(-1, LANES)
    anywhere = pl.BlockSpec(memory_space=pl.ANY)
    near = pl.BlockSpec(memory_space=pltpu.VMEM)
    table = pl.BlockSpec(memory_space=pltpu.SMEM)
    dma = pltpu.SemaphoreType.DMA
    cuts = len(cut_of(groups, capacity))
    steps = len(schedule(groups, chunks, cuts))
    half = jnp.bfloat16
    tile = ROWS * lanes
    scratch = (
        2 * 3 * slots * tile * 4
        + chunks * 2 * 3 * length * tile * 2
        + chunks * slots * tile * 2 * (2 + 3 * (chips - 1))
    )
    whole = pltpu.VMEM((length, rows, lanes), jnp.float32)
    *results, routed = pl.pallas_call(
        functools.partial(exchange_kernel, groups, replicas, capacity, chunks),
        out_shape=(
            whole, whole, whole,
            pltpu.VMEM((length,) + grads.shape[2:], half),
            pltpu.SMEM((2 * lines, wide), jnp.int32),
        ),
        in_specs=[anywhere] * 5,
        out_specs=(near,) * 4 + (table,),
        scratch_shapes=[
            pltpu.VMEM((2 * lines, wide), jnp.int32),
            pltpu.VMEM(dest.shape, jnp.int32),
            [[pltpu.VMEM((slots, ROWS, lanes), jnp.float32)] * 3] * 2,
            pltpu.VMEM((chunks, 3, length, ROWS, lanes), half),
            [pltpu.VMEM((3, length, ROWS, lanes), half)] * chunks,
            [pltpu.VMEM((slots, ROWS, lanes), half)] * chunks,
            pltpu.VMEM((chunks, chips - 1, slots, ROWS, lanes), half),
            [pltpu.VMEM((slots, ROWS, lanes), half)] * chunks,
            pltpu.VMEM((chunks, chips - 1, slots, ROWS, lanes), half),
            [[pltpu.VMEM((slots, ROWS, lanes), half)] * (chips - 1)] * chunks,
            dma((2,)),
            dma((2, 3)),
            dma((1 + chunks * (chips - 1),)),
            dma((1,)),
            dma((3 * chunks + cuts - 1 if groups == LINE else chunks * groups,)),
            dma((chips,)),
            dma((1 + chunks * (chips - 1),)),
            dma((chips - 1,)),
            dma((chunks, chips - 1)),
            dma((chips,)),
            dma((steps, chips - 1)),
            dma((1,)),
            dma((chips - 1,)),
            dma((chips - 1,)),
            dma((chips - 1,)),
        ],
        compiler_params=pltpu.CompilerParams(
            collective_id=0, has_side_effects=True, vmem_limit_bytes=scratch + SPARE
        ),
        name="exchange",
    )(dest, weight, first, second, grads)
    shape = jax.ShapeDtypeStruct(weight.shape, jnp.float32)
    return pl.pallas_call(
        functools.partial(place_kernel, groups, capacity),
        out_shape=(shape, shape, shape, jax.ShapeDtypeStruct(grads.shape[1:], half)),
        in_specs=[table] + [anywhere] * 4,
        out_specs=(anywhere,) * 4,
        scratch_shapes=[dma((4,))],
        compiler_params=pltpu.CompilerParams(vmem_limit_bytes=SPARE),
        name="place",
    )(routed, *results)


def shards(master_weight, first_moment, second_moment, grads, dest_table):
    groups = lax.axis_size("tensor")
    slots = master_weight.shape[0]
    capacity = 2 * ((slots + 2 * groups - 1) // (2 * groups))
    replicas = lax.axis_size("dp")
    return exchange(
        dest_table, master_weight, first_moment, second_moment, grads,
        groups, replicas, capacity,
    )


def solution(mesh):
    placed = (
        P(("section", "tensor"), "dp", None),
        P(("section", "tensor"), "dp", None),
        P(("section", "tensor"), "dp", None),
        P("dp", ("section", "tensor"), None, None),
        P(),
    )
    return jax.shard_map(
        shards,
        mesh=mesh,
        in_specs=placed,
        out_specs=(
            P(("section", "tensor"), "dp", None),
            P(("section", "tensor"), "dp", None),
            P(("section", "tensor"), "dp", None),
            P(("section", "tensor"), None, None),
        ),
        check_vma=False,
    )
```

```python
import functools
import math

import jax
import jax.numpy as jnp
from jax import lax
from jax.experimental import pallas as pl
from jax.experimental.pallas import tpu as pltpu
from jax.sharding import PartitionSpec as P

STEP = 10


learn_rate = 0.04
decay_rate = 1.5
beta_first = 0.9
beta_second = 0.95
epsilon = 1e-08


def adam_step(weight, first, second, grad):
    first_new = beta_first * first + (1.0 - beta_first) * grad
    second_new = beta_second * second + (1.0 - beta_second) * grad * grad
    first_hat = first_new * (1.0 / (1.0 - beta_first**STEP))
    second_hat = second_new * (1.0 / (1.0 - beta_second**STEP))
    weight_new = weight - learn_rate * (
        first_hat / (jnp.sqrt(second_hat) + epsilon) + decay_rate * weight
    )
    return (weight_new, first_new, second_new)


ROWS = 8
SCALE = 8192.0
SPARE = 512 * 1024
LANES = 128
HELD = 4096
LINE = 4
LAG = 4
DIRECT = 2
SHARES = 4
EARLY = 16
MESH = pl.DeviceIdType.MESH


def encode(weight):
    scaled = weight * SCALE
    square = scaled * scaled
    fourth = square * square
    return (scaled * jnp.abs(scaled) * square * fourth).astype(jnp.bfloat16)


def decode(code):
    wide = code.astype(jnp.float32)
    root = jnp.sqrt(jnp.sqrt(jnp.sqrt(jnp.abs(wide)))) * (1.0 / SCALE)
    return jnp.where(wide < 0.0, -root, root)


def loop(start, size, body):
    lax.fori_loop(0, size, lambda i, carry: (body(start + i), carry)[1], 0, unroll=math.gcd(size, 8))


def rows_from(flat, groups, slots):
    width = LANES * pl.cdiv(slots, LANES)
    found = []
    for group in range(groups):
        first, extra = divmod(group * slots, LANES)
        count = pl.cdiv(extra + slots, LANES)
        row = [flat[first + i : first + i + 1] for i in range(count)]
        row = jnp.concatenate(row, axis=1) if count > 1 else row[0]
        if extra:
            row = pltpu.roll(row, count * LANES - extra, 1)
        found.append(row[:, :width])
    return found


def lines_of(groups):
    return groups if groups % 4 == 0 else 8 * pl.cdiv(groups, 8)


def routes(flat, groups, slots, capacity, me):
    rows = rows_from(flat, groups, slots)
    width = rows[0].shape[1]
    lines = lines_of(groups)
    leaving = rows[0]
    for group in range(1, groups):
        leaving = jnp.where(me == group, rows[group], leaving)
    unused = [jnp.full_like(leaving, -1)] * (lines - groups)
    table = jnp.concatenate(rows + unused + [leaving] * groups + unused, axis=0)
    lane = lax.broadcasted_iota(jnp.int32, table.shape, 1)
    line = lax.broadcasted_iota(jnp.int32, table.shape, 0)
    table = table - jnp.where(line < lines, me, line - lines) * slots
    taken = (table >= 0) & (table < slots) & (lane < slots)
    taken = taken & (jnp.where(line < lines, line, line - lines) < groups)
    before = taken.astype(jnp.int32)
    step = 1
    while step < slots:
        total = before
        for shift in range(step, min(4 * step, slots), step):
            total = total + jnp.where(lane >= shift, pltpu.roll(before, shift, 1), 0)
        before = total
        step *= 4
    held = jnp.where(line < lines, table, lane) + 1 + HELD * (lane + 1 - before)
    held = jnp.where(taken, held, 0)
    reach = slots - capacity if groups * capacity == slots else slots - 1
    step = 1
    while step <= reach:
        digit = jnp.bitwise_and(held, 3 * HELD * step)
        total = jnp.where(digit == 0, held, 0)
        for shift in range(step, min(4 * step, reach + 1), step):
            moved = jnp.where(digit == HELD * shift, held, 0)
            total = total + pltpu.roll(moved, width - shift, 1)
        held = total
        step *= 4
    return jnp.bitwise_and(held, HELD - 1) - 1


def cut_of(groups, capacity):
    if groups == LINE and capacity % 8 == 0 and capacity > 32:
        return (capacity - 32, 16, 8, 8)
    return (capacity,)


def schedule(groups, chunks, cuts):
    if groups != LINE:
        return [(chunk, None, 0) for chunk in range(chunks)]
    last = chunks - 1
    timed = []
    for chunk in range(chunks):
        timed.append((chunk + 1.6, chunk, 0, 0))
        timed.append((chunk + 2.0, chunk, 1, 0))
        for role, when in ((2, 2.3), (3, 3.7)):
            count = cuts if chunk == last and role == 3 else 1
            late = last + 10.0 * role if chunk == last else chunk * 2.0 + when
            timed += [(late + piece, chunk, role, piece) for piece in range(count)]
    return [entry[1:] for entry in sorted(timed)]


def exchange_kernel(
    groups, replicas, capacity, chunks,
    dest, weight, first, second, grads,
    weight_new, first_new, second_new, weights, table,
    table_out, flat,
    raw, sent, got, own_here, own_far, twin_here, twin_far, far_here,
    table_sem, load_sem, own_sem, wide_send, wide_recv, twin_send, twin_recv, far_send, far_recv,
    last_send, last_recv, twin_last, relay_send, relay_recv, direct_send,
):
    slots, rows = weight.shape[0], weight.shape[1]
    me = lax.axis_index("tensor")
    mine = lax.axis_index("dp")
    chips = replicas // 2
    core = lax.rem(mine, 2)
    twin = mine + 1 - 2 * core
    across = range(1, chips)
    line = groups == LINE
    cuts = cut_of(groups, capacity)
    order = schedule(groups, chunks, len(cuts))
    straight = sum(cuts[-DIRECT:]) if line and len(cuts) > DIRECT else 0
    straight = 0 if straight * ROWS % rows else straight
    relayed = len(order) - (DIRECT if straight else 0)
    if line:
        side = me // 2
        near = me + 1 - 2 * lax.rem(me, 2)
        inner = lax.rem((me + 1) // 2, 2)
        opposite, facing = lax.rem(me + 2, 4), 3 - me
        first_target = inner * opposite + (1 - inner) * facing
        targets = [first_target, opposite + facing - first_target, near]
        sources = [me, near, 3 - 3 * side, 2 - side]
    else:
        targets = [lax.rem(me + k, groups) for k in range(1, groups)]
        sources = [lax.rem(me + groups - k, groups) for k in range(groups)]

    def far(k):
        return lax.rem(mine + 2 * k, replicas)

    def far_twin(k):
        return lax.rem(mine + 2 * k, replicas) + 1 - 2 * core

    def band(chunk, owner=None):
        if owner is None:
            return pl.ds(chunk * ROWS, ROWS)
        return pl.ds(pl.multiple_of(owner * rows + chunk * ROWS, ROWS), ROWS)

    def loads(chunk, kinds=range(3)):
        share = slots // SHARES if chunk == 0 and slots % SHARES == 0 else slots
        return [
            pltpu.make_async_copy(
                (weight, first, second)[k].at[pl.ds(begin, share), band(chunk), :],
                raw[chunk % 2][k].at[pl.ds(begin, share)],
                load_sem.at[chunk % 2, k],
            )
            for k in kinds
            for begin in range(0, slots, share)
        ]

    def loaded(chunk, k):
        pltpu.make_async_copy(raw[chunk % 2][k], raw[chunk % 2][k], load_sem.at[chunk % 2, k]).wait()

    def cut(chunk, piece, split):
        if chunk == chunks - 1 and split:
            return sum(cuts[:piece]), cuts[piece]
        return 0, capacity

    def slot(chunk, role, piece):
        last = chunks - 1
        return 3 * chunk + role - 1 + (piece if role == 3 and chunk == last else 0)

    def slot_there(chunk, piece, target):
        if not line:
            return chunk * groups + me
        if target is near:
            return slot(chunk, 1, 0)
        return slot(chunk, 2, 0) + inner * (1 + piece)

    def slot_here(chunk, role, piece, source):
        return slot(chunk, role, piece) if line else chunk * groups + source

    def wide(chunk, piece, split, source, target, place=0, kinds=slice(None), extent=None):
        begin, size = extent or cut(chunk, piece, split)
        return pltpu.make_async_remote_copy(
            src_ref=sent.at[chunk, kinds, pl.ds(target * capacity + begin, size)],
            dst_ref=got[chunk].at[kinds, pl.ds(source * capacity + begin, size)],
            send_sem=wide_send.at[0],
            recv_sem=wide_recv.at[place],
            device_id={"tensor": target},
            device_id_type=MESH,
        )

    def own_far_load(chunk, k):
        return pltpu.make_async_copy(
            grads.at[0, :, band(chunk, far(k)), :],
            own_far.at[chunk, k - 1],
            own_sem.at[1 + chunk * (chips - 1) + k - 1],
        )

    def own_here_load(chunk):
        return pltpu.make_async_copy(
            grads.at[0, :, band(chunk, mine), :], own_here[chunk], own_sem.at[0]
        )

    def grad_loads(chunk):
        return [own_far_load(chunk, k) for k in across] + [own_here_load(chunk)]

    def twin_copy(chunk, k):
        return pltpu.make_async_remote_copy(
            src_ref=grads.at[0, :, band(chunk, far_twin(k)), :],
            dst_ref=twin_far.at[chunk, k - 1] if k else twin_here[chunk],
            send_sem=twin_send.at[k],
            recv_sem=twin_recv.at[1 + chunk * (chips - 1) + k - 1 if k else 0],
            device_id={"dp": twin},
            device_id_type=MESH,
        )

    def far_copy(chunk, k):
        return pltpu.make_async_remote_copy(
            src_ref=own_far.at[chunk, k - 1],
            dst_ref=far_here[chunk][chips - k - 1],
            send_sem=far_send.at[k - 1],
            recv_sem=far_recv.at[chunk, chips - k - 1],
            device_id={"dp": far(k)},
            device_id_type=MESH,
        )

    def far_wait(chunk, k):
        return pltpu.make_async_remote_copy(
            src_ref=own_far.at[chunk, chips - k - 1],
            dst_ref=far_here[chunk][k - 1],
            send_sem=far_send.at[chips - k - 1],
            recv_sem=far_recv.at[chunk, k - 1],
            device_id={"dp": far(k)},
            device_id_type=MESH,
        )

    def extent(entry):
        chunk, role, piece = entry
        if role is None:
            return 0, groups * capacity
        begin, size = cut(chunk, piece, role > 2)
        return sources[role] * capacity + begin, size

    def rows_of(entry):
        if entry[1] is None:
            return [(source, 0, capacity) for source in range(groups)]
        return [(sources[entry[1]], *cut(entry[0], entry[2], entry[1] > 2))]

    def spread(step, owner, target, send, recv):
        start, size = extent(order[step])
        here = weights.at[pl.ds(start, size), band(order[step][0], owner), :]
        return pltpu.make_async_remote_copy(
            src_ref=here,
            dst_ref=here,
            send_sem=send,
            recv_sem=recv,
            device_id={"dp": target},
            device_id_type=MESH,
        )

    def far_spread(step, k):
        return spread(step, mine, far(k), last_send.at[k], last_recv.at[step, chips - k - 1])

    def twin_spread(step):
        return spread(step, mine, twin, last_send.at[0], twin_last.at[0])

    def relay(step, k):
        return spread(step, far(k), twin, relay_send.at[k - 1], relay_recv.at[k - 1])

    def direct_spread(step, k):
        return spread(step, mine, far_twin(k), direct_send.at[k - 1], relay_recv.at[chips - k - 1])

    def whole(owner, send, recv):
        here = weights.at[:, pl.ds(pl.multiple_of(owner * rows, ROWS), rows), :]
        return pltpu.make_async_remote_copy(
            src_ref=here,
            dst_ref=here,
            send_sem=send,
            recv_sem=recv,
            device_id={"dp": twin},
            device_id_type=MESH,
        )

    def every(ref, send, recv):
        return pltpu.make_async_remote_copy(
            src_ref=ref, dst_ref=ref, send_sem=send, recv_sem=recv,
            device_id={"dp": twin}, device_id_type=MESH,
        )

    def start(copies):
        for copy in copies:
            copy.start()

    fetch = pltpu.make_async_copy(dest, flat, table_sem.at[0])
    fetch.start()
    barrier = pltpu.get_barrier_semaphore()
    for target in targets:
        pl.semaphore_signal(barrier, inc=1, device_id={"tensor": target}, device_id_type=MESH)
    pl.semaphore_signal(barrier, inc=1, device_id={"dp": twin}, device_id_type=MESH)
    for k in across:
        pl.semaphore_signal(barrier, inc=1, device_id={"dp": far(k)}, device_id_type=MESH)
    half = table_out.shape[0] // 2
    start(loads(0, [0]))
    fetch.wait()
    table_out[...] = routes(flat[...], groups, slots, capacity, me)[:, : table_out.shape[1]]
    copy = pltpu.make_async_copy(table_out, table, table_sem.at[1])
    copy.start()
    copy.wait()
    loaded(0, 0)
    start(loads(0, [1, 2]))

    def pack(chunk, target, to_got=False, kinds=range(3), extent=(0, capacity)):
        def one(i):
            s = jnp.maximum(table[half + target, i], 0)
            j = target * capacity + i
            for k in kinds:
                value = raw[chunk % 2][k][s]
                value = encode(value) if k == 0 else value.astype(jnp.bfloat16)
                if to_got:
                    got[chunk][k, j] = value
                else:
                    sent[chunk, k, j] = value

        loop(*extent, one)

    waiting = []

    def send(copies):
        start(waiting)
        waiting[:] = copies

    for chunk in range(chunks):
        if chunk:
            for k in range(3):
                loaded(chunk, k)
        split = chunk == chunks - 1 and len(cuts) > 1
        for i, target in enumerate(targets):
            if chunk == 0 and i == 0:
                for k in range(3):
                    if k:
                        loaded(0, k)
                    early = EARLY if k == 0 and capacity > EARLY and not split else capacity
                    pack(0, target, kinds=(k,), extent=(0, early))
                    if k == 0:
                        pl.semaphore_wait(barrier, groups - 1 + chips)
                        start([twin_copy(0, i) for i in reversed(range(chips))])
                    if not split:
                        there = slot_there(0, 0, target)
                        reach = (0, early)
                        send([wide(0, 0, False, me, target, there, pl.ds(k, 1), reach)])
                        if k == 0:
                            send([])
                        if early < capacity:
                            reach = (early, capacity - early)
                            pack(0, target, kinds=(k,), extent=reach)
                            send([wide(0, 0, False, me, target, there, pl.ds(k, 1), reach)])
                for other in range(chunks):
                    start(grad_loads(other))
                if chunks > 1:
                    start(loads(1))
                for other in range(1, chunks):
                    start([twin_copy(other, k) for k in reversed(range(chips))])
                continue
            pack(chunk, target)
            if not split:
                send([wide(chunk, 0, False, me, target, slot_there(chunk, 0, target))])
        if split:
            send(
                [wide(chunk, 0, False, me, targets[-1], slot_there(chunk, 0, targets[-1]))]
                + [
                    wide(chunk, i, True, me, target, slot_there(chunk, i, target))
                    for i in range(len(cuts))
                    for target in targets[:-1]
                ]
            )
        pack(chunk, me, True)
        if chunk + 2 < chunks:
            start(loads(chunk + 2))
        send([])
        for k in across:
            own_far_load(chunk, k).wait()
            twin_copy(chunk, k).wait_recv()

            def join(s, chunk=chunk, k=k):
                total = own_far[chunk, k - 1, s].astype(jnp.float32) + twin_far[
                    chunk, k - 1, s
                ].astype(jnp.float32)
                own_far[chunk, k - 1, s] = total.astype(jnp.bfloat16)

            loop(0, slots, join)
            far_copy(chunk, k).start()

    def far_got(step, k):
        return spread(step, far(k), twin, relay_send.at[k - 1], last_recv.at[step, k - 1])

    def pass_on(step):
        for k in across:
            far_got(step, k).wait_recv()
            relay(step, k).start()

    pltpu.make_async_copy(own_far.at[:, 0], own_far.at[:, 0], own_sem.at[0]).wait()
    every(twin_far.at[:, 0], twin_send.at[0], twin_recv.at[0]).wait_recv()
    ready = set()
    behind = []
    for step, entry in enumerate(order):
        chunk, role, piece = entry
        if chunk not in ready:
            ready.add(chunk)
            for k in across:
                far_wait(chunk, k).wait_recv()
        if role is None:
            for source in sources[1:]:
                wide(chunk, 0, False, source, me, slot_here(chunk, 0, 0, source)).wait_recv()
        elif role > 0:
            place = slot_here(chunk, role, piece, sources[role])
            wide(chunk, piece, role > 2, sources[role], me, place).wait_recv()

        def update(source, i, chunk=chunk):
            p = jnp.maximum(table[source, i], 0)
            j = source * capacity + i
            grad = own_here[chunk][p].astype(jnp.float32) + twin_here[chunk][p].astype(jnp.float32)
            for k in across:
                grad = grad + far_here[chunk][k - 1][p].astype(jnp.float32)
            weight_here, first_here, second_here = adam_step(
                decode(got[chunk][0, j]),
                got[chunk][1, j].astype(jnp.float32),
                got[chunk][2, j].astype(jnp.float32),
                grad * (1.0 / replicas),
            )
            weights[j, band(chunk, mine)] = weight_here.astype(jnp.bfloat16)
            weight_new[j, band(chunk)] = weight_here
            first_new[j, band(chunk)] = first_here
            second_new[j, band(chunk)] = second_here

        for source, begin, size in rows_of(entry):
            loop(begin, size, functools.partial(update, source))
        start([far_spread(step, k) for k in across])
        if step >= relayed:
            start([direct_spread(step, k) for k in across])
        else:
            behind.append(step)
        twin_spread(step).start()
        while len(behind) > (LAG if chunk < chunks - 1 else 1 if step >= relayed else 2):
            pass_on(behind.pop(0))
    for step in behind:
        pass_on(step)
    for step in range(relayed, len(order)):
        for k in across:
            far_got(step, k).wait_recv()

    whole(twin, last_send.at[0], twin_last.at[0]).wait_recv()
    for k in across:
        whole(far_twin(k), relay_send.at[k - 1], relay_recv.at[k - 1]).wait_recv()
    whole(mine, last_send.at[0], twin_last.at[0]).wait_send()
    for k in across:
        whole(mine, last_send.at[k], twin_last.at[0]).wait_send()
        passed = weights.at[pl.ds(0, groups * capacity - straight * ROWS // rows), pl.ds(0, rows)]
        every(passed, relay_send.at[k - 1], twin_last.at[0]).wait_send()
        if straight:
            passed = weights.at[pl.ds(0, straight), pl.ds(0, ROWS)]
            every(passed, direct_send.at[k - 1], twin_last.at[0]).wait_send()
        every(own_far.at[:, k - 1], far_send.at[k - 1], twin_last.at[0]).wait_send()
    for k in range(chips):
        every(twin_far.at[:, max(k - 1, 0)], twin_send.at[k], twin_last.at[0]).wait_send()
    gone = sent.at[:, :, pl.ds(0, (groups - 1) * capacity)]
    every(gone, wide_send.at[0], twin_last.at[0]).wait_send()


def place_kernel(
    groups, capacity, table, weight, first, second, weights,
    weight_new, first_new, second_new, weights_new, sem,
):
    slots = weight_new.shape[0]
    pairs = ((weight, weight_new), (first, first_new), (second, second_new), (weights, weights_new))

    def one(source, i):
        p = table[source, i]
        j = source * capacity + i

        def move():
            for k, (held, target) in enumerate(pairs):
                pltpu.make_async_copy(held.at[j], target.at[p], sem.at[k]).start()

        if groups * capacity == slots:
            move()
        else:
            pl.when(p >= 0)(move)

    for source in range(groups):
        loop(0, capacity, functools.partial(one, source))
    for k, (held, target) in enumerate(pairs):
        pltpu.make_async_copy(held.at[pl.ds(0, slots)], target, sem.at[k]).wait()


def exchange(dest_table, weight, first, second, grads, groups, replicas, capacity):
    slots, rows, lanes = weight.shape
    chunks = rows // ROWS
    chips = replicas // 2
    length = groups * capacity
    lines = lines_of(groups)
    wide = LANES * pl.cdiv(capacity, LANES)
    spare = -dest_table.shape[0] % LANES
    dest = jnp.pad(dest_table, (0, spare)) if spare else dest_table
    dest = dest.reshape(-1, LANES)
    anywhere = pl.BlockSpec(memory_space=pl.ANY)
    near = pl.BlockSpec(memory_space=pltpu.VMEM)
    table = pl.BlockSpec(memory_space=pltpu.SMEM)
    dma = pltpu.SemaphoreType.DMA
    cuts = len(cut_of(groups, capacity))
    steps = len(schedule(groups, chunks, cuts))
    half = jnp.bfloat16
    tile = ROWS * lanes
    scratch = (
        2 * 3 * slots * tile * 4
        + chunks * 2 * 3 * length * tile * 2
        + chunks * slots * tile * 2 * (2 + 3 * (chips - 1))
    )
    whole = pltpu.VMEM((length, rows, lanes), jnp.float32)
    *results, routed = pl.pallas_call(
        functools.partial(exchange_kernel, groups, replicas, capacity, chunks),
        out_shape=(
            whole, whole, whole,
            pltpu.VMEM((length,) + grads.shape[2:], half),
            pltpu.SMEM((2 * lines, wide), jnp.int32),
        ),
        in_specs=[anywhere] * 5,
        out_specs=(near,) * 4 + (table,),
        scratch_shapes=[
            pltpu.VMEM((2 * lines, wide), jnp.int32),
            pltpu.VMEM(dest.shape, jnp.int32),
            [[pltpu.VMEM((slots, ROWS, lanes), jnp.float32)] * 3] * 2,
            pltpu.VMEM((chunks, 3, length, ROWS, lanes), half),
            [pltpu.VMEM((3, length, ROWS, lanes), half)] * chunks,
            [pltpu.VMEM((slots, ROWS, lanes), half)] * chunks,
            pltpu.VMEM((chunks, chips - 1, slots, ROWS, lanes), half),
            [pltpu.VMEM((slots, ROWS, lanes), half)] * chunks,
            pltpu.VMEM((chunks, chips - 1, slots, ROWS, lanes), half),
            [[pltpu.VMEM((slots, ROWS, lanes), half)] * (chips - 1)] * chunks,
            dma((2,)),
            dma((2, 3)),
            dma((1 + chunks * (chips - 1),)),
            dma((1,)),
            dma((3 * chunks + cuts - 1 if groups == LINE else chunks * groups,)),
            dma((chips,)),
            dma((1 + chunks * (chips - 1),)),
            dma((chips - 1,)),
            dma((chunks, chips - 1)),
            dma((chips,)),
            dma((steps, chips - 1)),
            dma((1,)),
            dma((chips - 1,)),
            dma((chips - 1,)),
            dma((chips - 1,)),
        ],
        compiler_params=pltpu.CompilerParams(
            collective_id=0, has_side_effects=True, vmem_limit_bytes=scratch + SPARE
        ),
        name="exchange",
    )(dest, weight, first, second, grads)
    shape = jax.ShapeDtypeStruct(weight.shape, jnp.float32)
    return pl.pallas_call(
        functools.partial(place_kernel, groups, capacity),
        out_shape=(shape, shape, shape, jax.ShapeDtypeStruct(grads.shape[1:], half)),
        in_specs=[table] + [anywhere] * 4,
        out_specs=(anywhere,) * 4,
        scratch_shapes=[dma((4,))],
        compiler_params=pltpu.CompilerParams(vmem_limit_bytes=SPARE),
        name="place",
    )(routed, *results)


def shards(master_weight, first_moment, second_moment, grads, dest_table):
    groups = lax.axis_size("tensor")
    slots = master_weight.shape[0]
    capacity = 2 * ((slots + 2 * groups - 1) // (2 * groups))
    replicas = lax.axis_size("dp")
    return exchange(
        dest_table, master_weight, first_moment, second_moment, grads,
        groups, replicas, capacity,
    )


def solution(mesh):
    placed = (
        P(("section", "tensor"), "dp", None),
        P(("section", "tensor"), "dp", None),
        P(("section", "tensor"), "dp", None),
        P("dp", ("section", "tensor"), None, None),
        P(),
    )
    return jax.shard_map(
        shards,
        mesh=mesh,
        in_specs=placed,
        out_specs=(
            P(("section", "tensor"), "dp", None),
            P(("section", "tensor"), "dp", None),
            P(("section", "tensor"), "dp", None),
            P(("section", "tensor"), None, None),
        ),
        check_vma=False,
    )
```
